256 devices in a mesh: dp: 32 (over y, z), expert: 8 (over x, core).
Axes of the slice: x: 4, y: 4, z: 8, core: 2. Of those that a mesh axis runs over, the one named last changes fastest.
Arguments:
- tokens: bfloat16 [4096, 4096], P('dp', 'expert'), may hold values from -24 to 24
- expert_ids: int32 [4096, 8], P('dp'), may hold values from 0 to 63, all different within a row; in each aligned block of 128 rows (0 to 127, 128 to 255, ...) at most 20 rows name the same one
- route_weights: float32 [4096, 8], P('dp'), may hold values from 0.05 to 1
- gate_weight: bfloat16 [64, 1536, 4096], P('dp', 'expert'), may hold values from -0.09375 to 0.09375
- up_weight: bfloat16 [64, 1536, 4096], P('dp', 'expert'), may hold values from -0.09375 to 0.09375
- down_weight: bfloat16 [64, 1536, 4096], P('dp', None, 'expert'), may hold values from -0.15625 to 0.15625
Outputs:
- quant_out: bfloat16 [4096, 4096], P('dp', 'expert')
- float_out: float32 [4096, 4096], P('dp', 'expert')
The draws below stay inside these ranges and needn't reach their ends.
Inputs may be any that keep to these rules, and one draw needn't show every extreme that they name: `expert_ids`: each row names 8 different experts; every expert is named by some row; within the 128 rows of one index of dp no expert is named more than 20 times, and in every draw some expert is named exactly 20 times in some such block.
All inputs are finite; a program needn't handle non-finite values. Where the reference program divides by a largest or mean magnitude, that divisor is 1e-20 or more.
Results may differ from the reference program's by a relative error of at most 0.011.
Values may be sent and summed in bfloat16 or wider, within the bound.
A program may use at most 128 MiB of HBM per device.

```python
import math
from functools import partial
import jax
import jax.numpy as jnp
import numpy as np
from jax import lax

D = 4096
FF = 1536
TOPK = 8
EXPERTS = 64
TOK_DEV = 128
CAP = 20
TOKENS = 4096
N_DP = 32


def draw_tokens(key, part):
    key_scale, key_body = jax.random.split(jax.random.fold_in(key, 17), 2)
    channel_scale = jnp.exp(jax.random.uniform(key_scale, (1, D), jnp.float32, math.log(0.05), math.log(4.0)))
    values = jnp.clip(jax.random.normal(key_body, (TOKENS, D), jnp.float32), -6.0, 6.0) * channel_scale
    return values.astype(jnp.bfloat16)


def block_scale(rng, shape, pieces, smallest, largest):
    factor_of, own = 1.0, jax.random.fold_in(rng, 6)
    for dim, shards_of in pieces:
        steps = jnp.exp(jax.random.uniform(jax.random.fold_in(own, dim), (shards_of,), jnp.float32, smallest / len(pieces), largest / len(pieces)))
        factor_of = factor_of * jnp.repeat(steps, shape[dim] // shards_of).reshape([-1 if axis == dim else 1 for axis in range(len(shape))])
    return factor_of


def shared_out(stream_key, own, number, rows, amount, top, most, slope):
    ranking = jax.random.permutation(stream_key, amount)
    crowded, ordinary = portions_of(amount, rows * top, most, slope, True), portions_of(amount, rows * top, most, slope, False)
    places = jnp.arange(amount)

    def named(lengths, turn):
        used = int((lengths > 0).sum())
        fixed = max(1, used // 4)
        passed = fixed + (places - fixed + turn * (used - fixed)) % max(1, amount - fixed)
        return jnp.zeros((amount,), jnp.int32).at[ranking[jnp.where(places < fixed, places, passed)]].set(jnp.asarray(lengths, jnp.int32))

    lengths = jnp.where(number % 4 == 0, named(crowded, number // 4), named(ordinary, number - number // 4 - 1))
    mixed = jax.random.permutation(jax.random.fold_in(own, 3), amount)
    source_of, sink = mixed[0:amount // 2 * 2:2], mixed[1:amount // 2 * 2:2]
    room = jnp.minimum(lengths[source_of] - 1, most - lengths[sink]) // 2
    room = jnp.where((source_of == ranking[0]) | (sink == ranking[0]) | (lengths[sink] == 0), 0, jnp.maximum(room, 0))
    passed = jax.random.randint(jax.random.fold_in(own, 4), (amount // 2,), 0, 1 << 20) % (room + 1)
    lengths = lengths.at[source_of].add(-passed).at[sink].add(passed)
    labels = jnp.searchsorted(jnp.cumsum(lengths), jnp.arange(rows * top), side="right").astype(jnp.int32)
    grid = labels.reshape(top, rows).T
    grid = grid[jax.random.permutation(jax.random.fold_in(own, 1), rows)]
    turn = jax.random.randint(jax.random.fold_in(own, 2), (rows, 1), 0, top)
    return jnp.take_along_axis(grid, (jnp.arange(top)[None, :] + turn) % top, axis=1)


def portions_of(number_of, total, most, slope, full):
    portions = [(1 << 20) // math.isqrt(rank ** slope) + 1 for rank in range(1, number_of + 1)]
    largest = most if full else min(most, max(-(-total // number_of), total * portions[0] // sum(portions)))
    least = 1 if total - largest >= number_of - 1 else 0
    counts, surplus = [largest] + [least] * (number_of - 1), total - largest - least * (number_of - 1)
    while surplus > 0:
        movable = [i for i in range(1, number_of) if counts[i] < largest] or [i for i in range(1, number_of) if counts[i] < most]
        mass, remaining = sum([portions[i] for i in movable]), surplus
        for i in movable:
            addition = min(most - counts[i], max(1, remaining * portions[i] // mass), surplus)
            counts[i] = counts[i] + addition
            surplus = surplus - addition
    return np.array(counts)


def centred(stream_key, extent, spread, bound, cuts=(), kind=jnp.bfloat16):
    array = spread * jax.random.normal(stream_key, extent, jnp.float32)
    if cuts:
        array = array * block_scale(stream_key, extent, cuts, -0.22, 0.18)
    return jnp.clip(array, -bound, bound).astype(kind)


def setup_inputs(seed: int = 0) -> dict:
    streams_of = jax.random.split(jax.random.key(seed), 7)
    tokens = draw_tokens(jax.random.fold_in(streams_of[6], 71), 0)
    expert_ids_keys = jax.random.split(jax.random.fold_in(streams_of[1], 1), TOKENS // TOK_DEV)
    expert_ids_turns = jax.random.permutation(jax.random.fold_in(streams_of[1], 3), TOKENS // TOK_DEV)
    expert_ids = jax.vmap(lambda own, number: shared_out(jax.random.fold_in(streams_of[1], 2), own, number, TOK_DEV, EXPERTS, TOPK, CAP, 2))(expert_ids_keys, expert_ids_turns).reshape((TOKENS, TOPK))
    route_weights = jnp.clip(jnp.exp(math.log(1.0) - 2.9957323 * jax.random.uniform(streams_of[2], (TOKENS, TOPK), jnp.float32) ** block_scale(streams_of[2], (TOKENS, TOPK), ((0, 32),), -0.2, 0.2)), 0.05, 1.0)
    gate_weight = centred(streams_of[3], (EXPERTS, FF, D), D ** -0.5, 0.09375, ((0, 32), (1, 8)))
    up_weight = centred(streams_of[4], (EXPERTS, FF, D), D ** -0.5, 0.09375, ((0, 32), (1, 8)))
    down_weight = centred(streams_of[5], (EXPERTS, FF, D), FF ** -0.5, 0.15625, ((0, 32), (2, 8)))
    return dict(tokens=tokens, expert_ids=expert_ids, route_weights=route_weights, gate_weight=gate_weight, up_weight=up_weight, down_weight=down_weight)


TWO_PI = 6.283185307179586

def soft_level(values):
    return values - jnp.sin(TWO_PI * values) / TWO_PI

def fake_quant(values, reduce_axis, levels):
    peak_abs = lax.optimization_barrier(jnp.max(jnp.abs(values), axis=reduce_axis, keepdims=True)) + 1e-06
    return peak_abs / levels * soft_level(levels * values / peak_abs)

def slot_layout(expert_ids):
    source_ids = expert_ids.reshape(N_DP, TOK_DEV * TOPK)
    hit_mask = (source_ids[:, :, None] == jnp.arange(EXPERTS, dtype=jnp.int32)[None, None, :]).astype(jnp.int32)
    before = jnp.cumsum(hit_mask, axis=1) - hit_mask
    slot_index = lax.optimization_barrier(jnp.sum(before * hit_mask, axis=2)).astype(jnp.int32)
    source = jnp.arange(N_DP, dtype=jnp.int32)[:, None]
    position = source * (TOK_DEV * TOPK) + jnp.arange(TOK_DEV * TOPK, dtype=jnp.int32)[None, :]
    token_index = (position // TOPK).astype(jnp.int32)
    target = (source_ids * (N_DP * CAP) + source * CAP + slot_index).astype(jnp.int32)
    slot_table = jnp.full((EXPERTS * N_DP * CAP,), -1, jnp.int32).at[target.reshape(-1)].set(token_index.reshape(-1))
    return (target.reshape(TOKENS, TOPK), slot_table.reshape(EXPERTS, N_DP * CAP))

def expert_pass(tokens, operands):
    token_index, w_gate, w_up, w_down = operands
    present = token_index >= 0
    picked = jnp.take(tokens, jnp.maximum(token_index, 0), axis=0)
    rows = jnp.where(present[:, None], picked, jnp.zeros_like(picked))
    gate_float = jnp.dot(rows, w_gate.T, preferred_element_type=jnp.float32)
    up_float = jnp.dot(rows, w_up.T, preferred_element_type=jnp.float32)
    hidden_float = (jax.nn.silu(gate_float) * up_float).astype(jnp.bfloat16)
    out_float = jnp.dot(hidden_float, w_down, preferred_element_type=jnp.float32).astype(jnp.bfloat16)
    rows_wide = rows.astype(jnp.float32)
    act_peak = jnp.maximum(lax.optimization_barrier(jnp.max(jnp.abs(rows_wide), axis=0)), 1.0)
    weight_peak = jnp.maximum(lax.optimization_barrier(jnp.max(jnp.abs(w_gate.astype(jnp.float32)), axis=0)), lax.optimization_barrier(jnp.max(jnp.abs(w_up.astype(jnp.float32)), axis=0))) + 1e-06
    smooth = jnp.sqrt(act_peak / weight_peak)
    rows_quant = fake_quant(rows_wide / smooth[None, :], 1, 7.0).astype(jnp.bfloat16)
    gate_quant_w = fake_quant(w_gate.astype(jnp.float32) * smooth[None, :], 1, 7.0).astype(jnp.bfloat16)
    up_quant_w = fake_quant(w_up.astype(jnp.float32) * smooth[None, :], 1, 7.0).astype(jnp.bfloat16)
    gate_quant = jnp.dot(rows_quant, gate_quant_w.T, preferred_element_type=jnp.float32)
    up_quant = jnp.dot(rows_quant, up_quant_w.T, preferred_element_type=jnp.float32)
    hidden_quant = (jax.nn.silu(gate_quant) * up_quant).astype(jnp.bfloat16)
    hidden_quant = lax.optimization_barrier(hidden_quant)
    hidden_levels = fake_quant(hidden_quant.astype(jnp.float32), 1, 7.0).astype(jnp.bfloat16)
    down_quant_w = fake_quant(w_down.astype(jnp.float32), 0, 7.0).astype(jnp.bfloat16)
    out_quant = jnp.dot(hidden_levels, down_quant_w, preferred_element_type=jnp.float32).astype(jnp.bfloat16)
    return (out_quant, out_float)

def reference(tokens, expert_ids, route_weights, gate_weight, up_weight, down_weight):
    target, slot_table = slot_layout(expert_ids)
    out_quant, out_float = lax.map(partial(expert_pass, tokens), (slot_table, gate_weight, up_weight, down_weight))
    flat_quant = out_quant.reshape(EXPERTS * N_DP * CAP, D)
    flat_float = out_float.reshape(EXPERTS * N_DP * CAP, D)
    shares = route_weights / lax.optimization_barrier(jnp.sum(route_weights, axis=1, keepdims=True))

    def accumulate(carry, column):
        acc_quant, acc_float = carry
        index_col, share_col = column
        acc_quant = acc_quant + share_col[:, None] * jnp.take(flat_quant, index_col, axis=0).astype(jnp.float32)
        acc_float = acc_float + share_col[:, None] * jnp.take(flat_float, index_col, axis=0).astype(jnp.float32)
        return ((acc_quant, acc_float), None)
    start = (jnp.zeros((TOKENS, D), jnp.float32), jnp.zeros((TOKENS, D), jnp.float32))
    (acc_quant, acc_float), _ = lax.scan(accumulate, start, (target.T, shares.T))
    return (acc_quant.astype(jnp.bfloat16), acc_float)
```

```python
import functools

import jax
import jax.numpy as jnp
from jax import lax
from jax.experimental import pallas as pl
from jax.experimental.pallas import tpu as pltpu
from jax.sharding import PartitionSpec as P

MESH = pl.DeviceIdType.MESH
CAP = 20
HEAD = 16
REST = CAP - HEAD
BF = jnp.bfloat16
F32 = jnp.float32
COEF = (6.579714691987998, -12.986868688853527, 12.19161471791364, -6.570950351250938, 1.9706418898295621)
ROUND = 12582912.0


def soft_level(values):
    whole = (values + ROUND) - ROUND
    rest = values - whole
    square = rest * rest
    poly = COEF[4]
    for coef in COEF[3::-1]:
        poly = poly * square + coef
    return whole + (rest * square) * poly


def dot_nt(a, b):
    return lax.dot_general(a, b, (((1,), (1,)), ((), ())), preferred_element_type=F32)


def dot_nn(a, b):
    return lax.dot_general(a, b, (((1,), (0,)), ((), ())), preferred_element_type=F32)


def iota(shape, axis):
    return lax.broadcasted_iota(jnp.int32, shape, axis)


def layer_kernel(
    groups,
    ring,
    tok_ref,
    ids_t_ref,
    ids_ref,
    route_ref,
    gate_hbm,
    up_hbm,
    down_hbm,
    quant_ref,
    float_ref,
    tok,
    send_head,
    send_rest,
    rows,
    rest_in,
    weight,
    weight_q,
    down,
    down_q,
    rows_q,
    acc_float,
    acc_quant,
    hid_float,
    hid_quant,
    hid_level,
    peak_own,
    peak_in,
    smooth,
    inv_smooth,
    row_peak,
    row_mul,
    row_div,
    col_mul,
    col_div,
    mix_head,
    mix_rest,
    outf_head,
    outf_rest,
    outq_head,
    outq_rest,
    rest_acc,
    backf_head,
    backf_rest,
    backq_head,
    backq_rest,
    part,
    part_in,
    load_sem,
    swap_send,
    swap_recv,
    a2a_send,
    a2a_recv,
    small_send,
    small_recv,
    ring_send,
    ring_recv,
    ex_send,
    ex_recv,
):
    me = lax.axis_index("dp")
    seat = lax.axis_index("expert")
    x = seat // 2
    core = seat % 2
    width = tok_ref.shape[1]
    wide = 2 * width
    quarter = wide // 4
    hid = gate_hbm.shape[1]
    hid2 = 2 * hid
    count = groups * CAP
    half = count // 2
    n_head = groups * HEAD
    n_rest = groups * REST
    top = ids_ref.shape[1]
    toks = tok_ref.shape[0]
    lanes = min(512, wide)
    block = 128 if count % 128 == 0 else count
    n_block = count // block
    hidden_all = ring * hid2

    partner = (me, x * 2 + 1 - core)

    def along(k):
        return (me, lax.rem(x + k, ring) * 2 + core)

    def peer(k):
        return (lax.rem(me + k, groups), seat)

    loads = []
    for s in range(ring):
        for g, src in enumerate((gate_hbm, up_hbm)):
            loads.append(
                pltpu.make_async_copy(
                    src.at[core, :, pl.ds(s * wide, wide)],
                    weight.at[s, pl.ds(pl.multiple_of(g * hid2 + core * hid, 8), hid), :],
                    load_sem.at[2 * s + g],
                )
            )
    loads.append(
        pltpu.make_async_copy(
            down_hbm.at[core],
            down.at[:, pl.ds(pl.multiple_of(core * width, 128), width)],
            load_sem.at[2 * ring],
        )
    )
    loads[-1].start()
    for copy in loads[:-1]:
        copy.start()

    barrier = pltpu.get_barrier_semaphore()
    pl.semaphore_signal(barrier, inc=1, device_id=partner, device_id_type=MESH)
    for k in range(1, ring):
        pl.semaphore_signal(barrier, inc=1, device_id=along(k), device_id_type=MESH)

    def greet(k, carry):
        pl.semaphore_signal(barrier, inc=1, device_id=peer(k), device_id_type=MESH)
        return carry

    lax.fori_loop(1, groups, greet, 0)

    before = (iota((toks, toks), 0) < iota((toks, toks), 1)).astype(BF)
    row_id = iota((n_head, toks), 0)
    hit = jnp.zeros((n_head, toks), F32)
    wanted = (row_id // HEAD) * 2 + core
    for k in range(top):
        hit = hit + (ids_t_ref[k : k + 1, :] == wanted).astype(F32)
    slot = dot_nn(hit.astype(BF), before)
    pick_head = jnp.where(slot == (row_id % HEAD).astype(F32), hit, 0.0).astype(BF)
    pick_rest = jnp.where(slot == (HEAD + row_id % REST).astype(F32), hit, 0.0)
    part_id = (row_id // REST) % 4

    pl.semaphore_wait(barrier, 1 + (ring - 1) + (groups - 1))

    own_cols = pl.ds(pl.multiple_of(core * width, 128), width)
    tok_copy = pltpu.make_async_remote_copy(
        src_ref=tok_ref,
        dst_ref=tok.at[:, own_cols],
        send_sem=swap_send.at[0],
        recv_sem=swap_recv.at[0],
        device_id=partner,
        device_id_type=MESH,
    )
    tok_copy.start()
    tok[:, own_cols] = tok_ref[...]
    swaps = [
        pltpu.make_async_remote_copy(
            src_ref=down_hbm.at[1 - core],
            dst_ref=down.at[:, own_cols],
            send_sem=swap_send.at[1],
            recv_sem=swap_recv.at[1],
            device_id=partner,
            device_id_type=MESH,
        )
    ]
    for s in range(ring):
        for g, src in enumerate((gate_hbm, up_hbm)):
            swaps.append(
                pltpu.make_async_remote_copy(
                    src_ref=src.at[1 - core, :, pl.ds(s * wide, wide)],
                    dst_ref=weight.at[s, pl.ds(pl.multiple_of(g * hid2 + core * hid, 8), hid), :],
                    send_sem=swap_send.at[2 + 2 * s + g],
                    recv_sem=swap_recv.at[2 + 2 * s + g],
                    device_id=partner,
                    device_id_type=MESH,
                )
            )
    tok_copy.wait()
    for copy in swaps:
        copy.start()

    send_head[...] = dot_nn(pick_head, tok[...]).astype(BF)
    chosen = jnp.zeros((n_head, quarter), F32)
    for q in range(4):
        chosen = chosen + dot_nn(
            jnp.where(part_id == q, pick_rest, 0.0).astype(BF), tok[:, q * quarter : (q + 1) * quarter]
        )
    send_rest[...] = chosen.astype(BF)

    my_head = pl.ds(pl.multiple_of(me * HEAD, HEAD), HEAD)

    def exchange(number, src_head, src_rest, dst_head, dst_rest):
        def copies(k):
            to = pl.ds(pl.multiple_of(lax.rem(me + k, groups) * HEAD, HEAD), HEAD)
            return (
                pltpu.make_async_remote_copy(
                    src_ref=src_head.at[to, :],
                    dst_ref=dst_head.at[my_head, :],
                    send_sem=a2a_send.at[number, 0],
                    recv_sem=a2a_recv.at[number, 0],
                    device_id=peer(k),
                    device_id_type=MESH,
                ),
                pltpu.make_async_remote_copy(
                    src_ref=src_rest.at[to, :],
                    dst_ref=dst_rest.at[my_head, :],
                    send_sem=a2a_send.at[number, 1],
                    recv_sem=a2a_recv.at[number, 1],
                    device_id=peer(k),
                    device_id_type=MESH,
                ),
            )

        def begin(k, carry):
            for copy in copies(k):
                copy.start()
            return carry

        lax.fori_loop(1, groups, begin, 0)
        dst_head[my_head, :] = src_head[my_head, :]
        dst_rest[my_head, :] = src_rest[my_head, :]

        total = pl.ds(0, (groups - 1) * HEAD)

        def waiting(index, src, dst):
            return pltpu.make_async_remote_copy(
                src_ref=src.at[total, :],
                dst_ref=dst.at[total, :],
                send_sem=a2a_send.at[number, index],
                recv_sem=a2a_recv.at[number, index],
                device_id=peer(1),
                device_id_type=MESH,
            )

        return (waiting(0, src_head, dst_head), waiting(1, src_rest, dst_rest))

    slab = rows.at[x]
    sent = exchange(0, send_head, send_rest, slab, rest_in)

    ratio = route_ref[...]
    ratio = ratio / jnp.sum(ratio, axis=1, keepdims=True)
    lane_id = iota((toks, n_head), 1)
    wanted_t = (lane_id // HEAD) * 2 + core
    hit_t = jnp.zeros((toks, n_head), F32)
    share_t = jnp.zeros((toks, n_head), F32)
    for k in range(top):
        same = ids_ref[:, k : k + 1] == wanted_t
        hit_t = hit_t + same.astype(F32)
        share_t = share_t + jnp.where(same, ratio[:, k : k + 1], 0.0)
    before_t = (iota((toks, toks), 1) < iota((toks, toks), 0)).astype(BF)
    slot_t = dot_nn(before_t, hit_t.astype(BF))
    for which, ref in (
        ((lane_id % HEAD).astype(F32), mix_head),
        ((HEAD + lane_id % REST).astype(F32), mix_rest),
    ):
        value = jnp.where(slot_t == which, share_t, 0.0)
        high = value.astype(BF)
        ref[0:toks, :] = high
        ref[toks:, :] = (value - high.astype(F32)).astype(BF)

    loads[-1].wait()
    swaps[0].wait()
    for n in range(wide // lanes):
        cols = slice(n * lanes, (n + 1) * lanes)

        def down_peak(i, best):
            at = pl.ds(pl.multiple_of(i * 16, 16), 16)
            return jnp.maximum(best, jnp.abs(down[at, cols].astype(F32)))

        best = lax.fori_loop(0, hidden_all // 16, down_peak, jnp.zeros((16, lanes), F32))
        peak = jnp.max(best, axis=0, keepdims=True) + 1e-06
        col_mul[:, cols] = jnp.broadcast_to(7.0 / peak, (8, lanes))
        col_div[:, cols] = jnp.broadcast_to(peak / 7.0, (8, lanes))

        def down_level(i, carry):
            at = pl.ds(pl.multiple_of(i * 16, 16), 16)
            value = down[at, cols].astype(F32)
            mul = jnp.concatenate((col_mul[:, cols], col_mul[:, cols]), axis=0)
            div = jnp.concatenate((col_div[:, cols], col_div[:, cols]), axis=0)
            down_q[at, cols] = (div * soft_level(value * mul)).astype(BF)
            return carry

        lax.fori_loop(0, hidden_all // 16, down_level, 0)

    for s in range(ring):
        loads[2 * s].wait()
        loads[2 * s + 1].wait()
        swaps[1 + 2 * s].wait()
        swaps[2 + 2 * s].wait()
        for n in range(wide // lanes):
            cols = slice(n * lanes, (n + 1) * lanes)

            def weight_top(i, best):
                at = pl.ds(pl.multiple_of(i * 16, 16), 16)
                return jnp.maximum(best, jnp.abs(weight[s, at, cols].astype(F32)))

            best = lax.fori_loop(0, 2 * hid2 // 16, weight_top, jnp.zeros((16, lanes), F32))
            peak_own[s, :, cols] = jnp.broadcast_to(jnp.max(best, axis=0, keepdims=True), (8, lanes))

    def small(number, k, src, dst):
        return pltpu.make_async_remote_copy(
            src_ref=src,
            dst_ref=dst,
            send_sem=small_send.at[number, k - 1],
            recv_sem=small_recv.at[number, k - 1],
            device_id=along(k),
            device_id_type=MESH,
        )

    peak_copies = [
        small(0, k, peak_own.at[lax.rem(x + k, ring)], peak_in.at[k - 1]) for k in range(1, ring)
    ]
    for copy in peak_copies:
        copy.start()
    for copy in peak_copies:
        copy.wait()
    weight_peak = peak_own[x]
    for k in range(1, ring):
        weight_peak = jnp.maximum(weight_peak, peak_in[k - 1])

    for copy in sent:
        copy.wait_send()
        copy.wait_recv()
    spread = iota((n_rest, n_head), 1)
    home = iota((n_rest, n_head), 0)
    same_row = (spread // HEAD == home // REST) & (spread % REST == home % REST)
    for q in range(4):
        order = (same_row & ((spread // REST) % 4 == q)).astype(F32).astype(BF)
        slab[n_head:, q * quarter : (q + 1) * quarter] = dot_nn(order, rest_in[...]).astype(BF)

    for n in range(wide // lanes):
        cols = slice(n * lanes, (n + 1) * lanes)

        def act_top(i, best):
            at = pl.ds(pl.multiple_of(i * 16, 16), 16)
            return jnp.maximum(best, jnp.abs(rows[x, at, cols].astype(F32)))

        best = lax.fori_loop(0, count // 16, act_top, jnp.zeros((16, lanes), F32)) if count % 16 == 0 else jnp.abs(
            rows[x, :, cols].astype(F32)
        )
        act_peak = jnp.maximum(jnp.max(best, axis=0, keepdims=True), 1.0)
        value = jnp.sqrt(act_peak / (weight_peak[:, cols] + 1e-06))
        smooth[x, :, cols] = value
        inv_smooth[x, :, cols] = 1.0 / value
    smooth_copies = [small(1, k, smooth.at[x], smooth.at[x]) for k in range(1, ring)]
    for copy in smooth_copies:
        copy.start()

    eye = iota((block, block), 0) == iota((block, block), 1)
    top_rows = []
    for b in range(n_block):
        best = jnp.zeros((block, 128 if wide >= 128 else wide), F32)
        step = best.shape[1]
        for n in range(wide // step):
            cols = slice(n * step, (n + 1) * step)
            value = rows[x, b * block : (b + 1) * block, cols].astype(F32) * inv_smooth[x, 0:1, cols]
            best = jnp.maximum(best, jnp.abs(value))
        tall = jnp.max(best, axis=1, keepdims=True)
        top_rows.append(jnp.sum(jnp.where(eye, tall, 0.0), axis=0, keepdims=True))
    row_peak[x] = jnp.zeros((8, block), F32)
    for b in range(n_block):
        row_peak[x, b : b + 1, :] = top_rows[b]
    peak_rows = [small(2, k, row_peak.at[x], row_peak.at[x]) for k in range(1, ring)]
    for copy in peak_rows:
        copy.start()

    def hop(number, ref, way, step):
        mag = step // 2
        if way == 0:
            owner = lax.rem(x - mag + ring, ring)
            part_of = step % 2
            to = along(1)
        else:
            owner = lax.rem(x + mag, ring)
            part_of = 1 - step % 2
            to = along(ring - 1)
        at = pl.ds(part_of * half, half)
        return pltpu.make_async_remote_copy(
            src_ref=ref.at[owner, at, :],
            dst_ref=ref.at[owner, at, :],
            send_sem=ring_send.at[number, way, step],
            recv_sem=ring_recv.at[number, way, step],
            device_id=to,
            device_id_type=MESH,
        )

    def landed(number, ref, way, step):
        mag = 1 + step // 2
        if way == 0:
            owner = lax.rem(x - mag + ring, ring)
            part_of = step % 2
        else:
            owner = lax.rem(x + mag, ring)
            part_of = 1 - step % 2
        at = pl.ds(part_of * half, half)
        copy = pltpu.make_async_remote_copy(
            src_ref=ref.at[owner, at, :],
            dst_ref=ref.at[owner, at, :],
            send_sem=ring_send.at[number, way, step],
            recv_sem=ring_recv.at[number, way, step],
            device_id=along(1),
            device_id_type=MESH,
        )
        return copy, owner, part_of

    def launch(number, ref):
        for step in range(2):
            for way in range(2):
                hop(number, ref, way, step).start()

    launch(0, rows)

    for copy in smooth_copies:
        copy.wait()

    def weight_level(i, carry):
        at = pl.ds(pl.multiple_of(i * 16, 16), 16)
        best = jnp.zeros((16, lanes), F32)
        for s in range(ring):
            for n in range(wide // lanes):
                cols = slice(n * lanes, (n + 1) * lanes)
                best = jnp.maximum(best, jnp.abs(weight[s, at, cols].astype(F32) * smooth[s, 0:1, cols]))
        peak = jnp.max(best, axis=1, keepdims=True) + 1e-06
        mul = 7.0 / peak
        div = peak / 7.0
        for s in range(ring):
            for n in range(wide // lanes):
                cols = slice(n * lanes, (n + 1) * lanes)
                value = weight[s, at, cols].astype(F32) * smooth[s, 0:1, cols]
                weight_q[s, at, cols] = (div * soft_level(value * mul)).astype(BF)
        return carry

    lax.fori_loop(0, 2 * hid2 // 16, weight_level, 0)

    for copy in peak_rows:
        copy.wait()
    best_row = row_peak[0]
    for s in range(1, ring):
        best_row = jnp.maximum(best_row, row_peak[s])
    for s in range(ring):
        inv_smooth[s, :, :] = 1.0 / smooth[s]
    for b in range(n_block):
        flat = jnp.broadcast_to(best_row[b : b + 1, :], (block, block))
        tall = jnp.sum(jnp.where(eye, flat, 0.0), axis=1, keepdims=True) + 1e-06
        row_mul[b * block : (b + 1) * block, :] = jnp.broadcast_to(7.0 / tall, (block, 128))
        row_div[b * block : (b + 1) * block, :] = jnp.broadcast_to(tall / 7.0, (block, 128))

    acc_float[...] = jnp.zeros_like(acc_float)
    acc_quant[...] = jnp.zeros_like(acc_quant)

    strip = 16 if half % 16 == 0 else half

    def use(owner, part_of):
        at = pl.ds(part_of * half, half)
        acc_float[at, :] += dot_nt(rows[owner, at, :], weight[owner])

        def row_level(i, carry):
            here = pl.ds(part_of * half + i * strip, strip)
            out = pl.ds(i * strip, strip)
            mul = row_mul[here, 0:1]
            div = row_div[here, 0:1]
            for n in range(wide // lanes):
                cols = slice(n * lanes, (n + 1) * lanes)
                value = rows[owner, here, cols].astype(F32) * inv_smooth[owner, 0:1, cols]
                rows_q[out, cols] = (div * soft_level(value * mul)).astype(BF)
            return carry

        lax.fori_loop(0, half // strip, row_level, 0)
        acc_quant[at, :] += dot_nt(rows_q[...], weight_q[owner])

    def own_half(i, carry):
        use(x, i)
        return carry

    lax.fori_loop(0, 2, own_half, 0)

    def arrival(step, carry):
        for way in range(2):
            copy, owner, part_of = landed(0, rows, way, step)
            copy.wait_recv()

            @pl.when(step == 0)
            def _():
                hop(0, rows, way, 2).start()

            use(owner, part_of)
        return carry

    lax.fori_loop(0, 3, arrival, 0)

    def activate(acc, out):
        def piece(i, carry):
            at = pl.ds(pl.multiple_of(i * strip, strip), strip)
            gate = acc[at, 0:hid2]
            out[x, at, :] = (gate / (1.0 + jnp.exp(-gate)) * acc[at, hid2:]).astype(BF)
            return carry

        lax.fori_loop(0, count // strip, piece, 0)

    def relay(number, ref):
        for way in range(2):
            landed(number, ref, way, 0)[0].wait_recv()
            hop(number, ref, way, 2).start()

    def finish(number, ref):
        for step in range(1, 3):
            for way in range(2):
                landed(number, ref, way, step)[0].wait_recv()

    def drain(number, ref):
        for step in range(3):
            for way in range(2):
                hop(number, ref, way, step).wait_send()

    turn = iota((n_head, n_rest), 0)
    base = iota((n_head, n_rest), 1)
    back_row = (turn // HEAD == base // REST) & (turn % REST == base % REST)
    turn_part = (turn // REST) % 4

    def project(hidden, matrix, head, rest):
        rest_acc[...] = jnp.zeros_like(rest_acc)

        def piece(q, carry):
            cols = pl.ds(pl.multiple_of(q * quarter, quarter), quarter)
            total = dot_nn(hidden[0], matrix[0:hid2, cols])
            for s in range(1, ring):
                total = total + dot_nn(hidden[s], matrix[s * hid2 : (s + 1) * hid2, cols])
            total = total.astype(BF)
            head[:, cols] = total[:n_head]
            order = (back_row & (turn_part == q)).astype(F32).astype(BF)
            rest_acc[...] += dot_nn(order, total[n_head:])
            return carry

        lax.fori_loop(0, 4, piece, 0)
        rest[...] = rest_acc[...].astype(BF)

    activate(acc_float, hid_float)
    launch(1, hid_float)
    activate(acc_quant, hid_quant)
    relay(1, hid_float)
    launch(2, hid_quant)
    finish(1, hid_float)
    project(hid_float, down, outf_head, outf_rest)
    sent_float = exchange(1, outf_head, outf_rest, backf_head, backf_rest)
    relay(2, hid_quant)
    finish(2, hid_quant)

    def level(i, carry):
        at = pl.ds(pl.multiple_of(i * strip, strip), strip)
        best = jnp.zeros((strip, hid2), F32)
        for s in range(ring):
            best = jnp.maximum(best, jnp.abs(hid_quant[s, at, :].astype(F32)))
        peak = jnp.max(best, axis=1, keepdims=True) + 1e-06
        mul = 7.0 / peak
        div = peak / 7.0
        for s in range(ring):
            value = hid_quant[s, at, :].astype(F32)
            hid_level[s, at, :] = (div * soft_level(value * mul)).astype(BF)
        return carry

    lax.fori_loop(0, count // strip, level, 0)
    project(hid_level, down_q, outq_head, outq_rest)
    sent_quant = exchange(2, outq_head, outq_rest, backq_head, backq_rest)

    def combine(number, head, rest):
        mixed = dot_nn(mix_head[...], head[...])
        mixed = mixed[:toks] + mixed[toks:]
        quarter_of = (iota((2 * toks, n_head), 1) // REST) % 4
        for q in range(4):
            weights = jnp.where(quarter_of == q, mix_rest[...].astype(F32), 0.0).astype(BF)
            extra = dot_nn(weights, rest[...])
            cols = slice(q * quarter, (q + 1) * quarter)
            first = (q * quarter) // width
            inner = q * quarter - first * width
            part[number, first, :, inner : inner + quarter] = mixed[:, cols] + extra[:toks] + extra[toks:]
        copy = pltpu.make_async_remote_copy(
            src_ref=part.at[number, 1 - core],
            dst_ref=part_in.at[number],
            send_sem=ex_send.at[number],
            recv_sem=ex_recv.at[number],
            device_id=partner,
            device_id_type=MESH,
        )
        copy.start()
        return copy

    for copy in sent_float:
        copy.wait_recv()
    half_float = combine(0, backf_head, backf_rest)
    half_float.wait()
    float_ref[...] = part[0, core] + part_in[0]
    for copy in sent_quant:
        copy.wait_recv()
    half_quant = combine(1, backq_head, backq_rest)

    for copy in sent_float:
        copy.wait_send()
    for copy in sent_quant:
        copy.wait_send()
    for number, ref in enumerate((rows, hid_float, hid_quant)):
        drain(number, ref)
    half_quant.wait()
    quant_ref[...] = (part[1, core] + part_in[1]).astype(BF)


def solution(mesh):
    groups = mesh.shape["dp"]
    ring = mesh.shape["expert"] // 2

    def on_device(tokens, expert_ids, route_weights, gate_weight, up_weight, down_weight):
        toks, width = tokens.shape
        wide = 2 * width
        quarter = wide // 4
        hid = gate_weight.shape[1]
        hid2 = 2 * hid
        count = groups * CAP
        half = count // 2
        n_head = groups * HEAD
        hidden_all = ring * hid2
        block = 128 if count % 128 == 0 else count
        vmem = pltpu.VMEM
        dma = pltpu.SemaphoreType.DMA
        here = pl.BlockSpec(memory_space=pltpu.VMEM)
        away = pl.BlockSpec(memory_space=pl.ANY)
        return pl.pallas_call(
            functools.partial(layer_kernel, groups, ring),
            name="moe_layer",
            out_shape=(
                jax.ShapeDtypeStruct((toks, width), BF),
                jax.ShapeDtypeStruct((toks, width), F32),
            ),
            in_specs=[here, here, here, here, away, away, away],
            out_specs=(here, here),
            scratch_shapes=[
                vmem((toks, wide), BF),
                vmem((n_head, wide), BF),
                vmem((n_head, quarter), BF),
                vmem((ring, count, wide), BF),
                vmem((n_head, quarter), BF),
                vmem((ring, 2 * hid2, wide), BF),
                vmem((ring, 2 * hid2, wide), BF),
                vmem((hidden_all, wide), BF),
                vmem((hidden_all, wide), BF),
                vmem((half, wide), BF),
                vmem((count, 2 * hid2), F32),
                vmem((count, 2 * hid2), F32),
                vmem((ring, count, hid2), BF),
                vmem((ring, count, hid2), BF),
                vmem((ring, count, hid2), BF),
                vmem((ring, 8, wide), F32),
                vmem((ring - 1, 8, wide), F32),
                vmem((ring, 8, wide), F32),
                vmem((ring, 8, wide), F32),
                vmem((ring, 8, block), F32),
                vmem((count, 128), F32),
                vmem((count, 128), F32),
                vmem((8, wide), F32),
                vmem((8, wide), F32),
                vmem((2 * toks, n_head), BF),
                vmem((2 * toks, n_head), BF),
                vmem((n_head, wide), BF),
                vmem((n_head, quarter), BF),
                vmem((n_head, wide), BF),
                vmem((n_head, quarter), BF),
                vmem((n_head, quarter), F32),
                vmem((n_head, wide), BF),
                vmem((n_head, quarter), BF),
                vmem((n_head, wide), BF),
                vmem((n_head, quarter), BF),
                vmem((2, 2, toks, width), F32),
                vmem((2, toks, width), F32),
                dma((2 * ring + 1,)),
                dma((2 + 2 * ring,)),
                dma((2 + 2 * ring,)),
                dma((3, 2)),
                dma((3, 2)),
                dma((3, ring - 1)),
                dma((3, ring - 1)),
                dma((3, 2, 3)),
                dma((3, 2, 3)),
                dma((2,)),
                dma((2,)),
            ],
            compiler_params=pltpu.CompilerParams(
                collective_id=0, has_side_effects=True, vmem_limit_bytes=64 * 1024 * 1024 - 128 * 1024
            ),
        )(
            tokens,
            expert_ids.T,
            expert_ids,
            route_weights,
            gate_weight,
            up_weight,
            down_weight,
        )

    in_specs = (
        P("dp", "expert"),
        P("dp", None),
        P("dp", None),
        P("dp", "expert", None),
        P("dp", "expert", None),
        P("dp", None, "expert"),
    )
    out_specs = (P("dp", "expert"), P("dp", "expert"))
    return jax.shard_map(
        on_device, mesh=mesh, in_specs=in_specs, out_specs=out_specs, check_vma=False
    )
```

```python
import functools

import jax
import jax.numpy as jnp
from jax import lax
from jax.experimental import pallas as pl
from jax.experimental.pallas import tpu as pltpu
from jax.sharding import PartitionSpec as P

MESH = pl.DeviceIdType.MESH
CAP = 20
HEAD = 16
REST = CAP - HEAD
BF = jnp.bfloat16
F32 = jnp.float32
COEF = (6.5788915972740805, -12.960054087409885, 11.90224462767755, -5.297839452865238)
ROUND = 12582912.0


def soft_level(values):
    whole = (values + ROUND) - ROUND
    rest = values - whole
    square = rest * rest
    poly = COEF[-1]
    for coef in COEF[-2::-1]:
        poly = poly * square + coef
    return whole + (rest * square) * poly


def dot_nt(a, b):
    return lax.dot_general(a, b, (((1,), (1,)), ((), ())), preferred_element_type=F32)


def dot_nn(a, b):
    return lax.dot_general(a, b, (((1,), (0,)), ((), ())), preferred_element_type=F32)


def iota(shape, axis):
    return lax.broadcasted_iota(jnp.int32, shape, axis)


def layer_kernel(
    groups,
    ring,
    tok_ref,
    ids_t_ref,
    route_ref,
    gate_hbm,
    up_hbm,
    down_hbm,
    quant_ref,
    float_ref,
    tok,
    send_head,
    send_rest,
    rows,
    rest_in,
    weight,
    weight_q,
    down,
    down_q,
    rows_q,
    acc_float,
    acc_quant,
    hid_float,
    hid_quant,
    hid_level,
    peak_own,
    peak_in,
    smooth,
    inv_smooth,
    row_peak,
    row_mul,
    row_div,
    level_div,
    col_mul,
    col_div,
    top_send,
    top_in,
    mix_head,
    mix_rest,
    outf_head,
    outf_rest,
    outq_head,
    outq_rest,
    rest_acc,
    backf_head,
    backf_rest,
    backq_head,
    backq_rest,
    part,
    part_in,
    load_sem,
    swap_send,
    swap_recv,
    a2a_send,
    a2a_recv,
    small_send,
    small_recv,
    ring_send,
    ring_recv,
    ex_send,
    ex_recv,
):
    me = lax.axis_index("dp")
    seat = lax.axis_index("expert")
    x = seat // 2
    core = seat % 2
    width = tok_ref.shape[1]
    wide = 2 * width
    quarter = wide // 4
    hid = gate_hbm.shape[1]
    hid2 = 2 * hid
    count = groups * CAP
    half = count // 2
    n_head = groups * HEAD
    gh = groups // 2
    half_head = gh * HEAD
    piece_rows = half // 2
    top = ids_t_ref.shape[0]
    toks = tok_ref.shape[0]
    lanes = min(512, wide)
    block = 128 if count % 128 == 0 else count
    n_block = count // block
    hidden_all = ring * hid2

    partner = (me, x * 2 + 1 - core)

    def along(k):
        return (me, lax.rem(x + k, ring) * 2 + core)

    def peer(k):
        return (lax.rem(me + k, groups), seat)

    loads = []
    for s in range(ring):
        for g, src in enumerate((gate_hbm, up_hbm)):
            loads.append(
                pltpu.make_async_copy(
                    src.at[core, :, pl.ds(s * wide, wide)],
                    weight.at[s, pl.ds(pl.multiple_of(g * hid2 + core * hid, 8), hid), :],
                    load_sem.at[2 * s + g],
                )
            )
    loads.append(
        pltpu.make_async_copy(
            down_hbm.at[core],
            down.at[:, pl.ds(pl.multiple_of(core * width, 128), width)],
            load_sem.at[2 * ring],
        )
    )
    loads[-1].start()
    for copy in loads[:-1]:
        copy.start()

    barrier = pltpu.get_barrier_semaphore()
    pl.semaphore_signal(barrier, inc=1, device_id=partner, device_id_type=MESH)
    for k in range(1, ring):
        pl.semaphore_signal(barrier, inc=1, device_id=along(k), device_id_type=MESH)

    def greet(k, carry):
        pl.semaphore_signal(barrier, inc=1, device_id=peer(k), device_id_type=MESH)
        return carry

    lax.fori_loop(1, groups, greet, 0)

    before = (iota((toks, toks), 0) < iota((toks, toks), 1)).astype(BF)
    row_id = iota((n_head, toks), 0)
    hit = jnp.zeros((n_head, toks), F32)
    wanted = (row_id // HEAD) * 2 + core
    share = jnp.zeros((n_head, toks), F32)
    ratio = route_ref[...]
    ratio = ratio / jnp.sum(ratio, axis=0, keepdims=True)
    for k in range(top):
        same = ids_t_ref[k : k + 1, :] == wanted
        hit = hit + same.astype(F32)
        share = share + jnp.where(same, ratio[k : k + 1, :], 0.0)
    slot = dot_nn(hit.astype(BF), before)
    pick_head = jnp.where(slot == (row_id % HEAD).astype(F32), hit, 0.0).astype(BF)
    pick_rest = jnp.where(slot == (HEAD + row_id % REST).astype(F32), hit, 0.0)
    part_id = (row_id // REST) % 4
    hit_group = jnp.zeros((groups, toks), F32)
    wanted = iota((groups, toks), 0) * 2 + core
    for k in range(top):
        hit_group = hit_group + (ids_t_ref[k : k + 1, :] == wanted).astype(F32)
    slot_group = dot_nn(hit_group.astype(BF), before)
    pick_all = jnp.concatenate(
        [jnp.where(slot_group == float(n), hit_group, 0.0).astype(BF) for n in range(CAP)], axis=0
    )
    tiles = wide // 128
    eighth = quarter // 2
    middle = wide // 2

    pl.semaphore_wait(barrier, 1 + (ring - 1) + (groups - 1))

    own_cols = pl.ds(pl.multiple_of(core * width, 128), width)
    tok_copy = pltpu.make_async_remote_copy(
        src_ref=tok_ref,
        dst_ref=tok.at[:, own_cols],
        send_sem=swap_send.at[0],
        recv_sem=swap_recv.at[0],
        device_id=partner,
        device_id_type=MESH,
    )
    tok_copy.start()
    tok[:, own_cols] = tok_ref[...]
    swaps = [
        pltpu.make_async_remote_copy(
            src_ref=down_hbm.at[1 - core],
            dst_ref=down.at[:, own_cols],
            send_sem=swap_send.at[1],
            recv_sem=swap_recv.at[1],
            device_id=partner,
            device_id_type=MESH,
        )
    ]
    for s in range(ring):
        for g, src in enumerate((gate_hbm, up_hbm)):
            swaps.append(
                pltpu.make_async_remote_copy(
                    src_ref=src.at[1 - core, :, pl.ds(s * wide, wide)],
                    dst_ref=weight.at[s, pl.ds(pl.multiple_of(g * hid2 + core * hid, 8), hid), :],
                    send_sem=swap_send.at[2 + 2 * s + g],
                    recv_sem=swap_recv.at[2 + 2 * s + g],
                    device_id=partner,
                    device_id_type=MESH,
                )
            )
    tok_copy.wait()
    for copy in swaps:
        copy.start()

    every = jnp.abs(dot_nn(pick_all, tok[...]))
    highest = every[0:groups]
    for n in range(1, CAP):
        highest = jnp.maximum(highest, every[n * groups : (n + 1) * groups])
    for n in range(tiles):
        top_send[pl.ds(n, groups, stride=tiles), :] = highest[:, n * 128 : (n + 1) * 128]

    def top_at(g):
        return pl.ds(pl.multiple_of(g * tiles, tiles), tiles)

    def send_top(k, carry):
        pltpu.make_async_remote_copy(
            src_ref=top_send.at[top_at(lax.rem(me + k, groups)), :],
            dst_ref=top_in.at[top_at(me), :],
            send_sem=a2a_send.at[4, 0],
            recv_sem=a2a_recv.at[4, 0],
            device_id=peer(k),
            device_id_type=MESH,
        ).start()
        return carry

    lax.fori_loop(1, groups, send_top, 0)
    top_in[top_at(me), :] = top_send[top_at(me), :]

    send_head[...] = dot_nn(pick_head, tok[...]).astype(BF)
    chosen = jnp.zeros((n_head, quarter), F32)
    for q in range(4):
        pair = jnp.concatenate(
            (
                tok[:, q * eighth : (q + 1) * eighth],
                tok[:, middle + q * eighth : middle + (q + 1) * eighth],
            ),
            axis=1,
        )
        chosen = chosen + dot_nn(jnp.where(part_id == q, pick_rest, 0.0).astype(BF), pair)
    send_rest[...] = chosen.astype(BF)

    def at_group(g):
        return pl.ds(pl.multiple_of(g * HEAD, HEAD), HEAD)

    def split_group(g):
        return pl.ds(pl.multiple_of((g % 2) * half_head + (g // 2) * HEAD, HEAD), HEAD)

    def landing_group(g):
        return pl.ds(pl.multiple_of((g % 2) * half + (g // 2) * HEAD, HEAD), HEAD)

    def remote(number, index, src, dst, k):
        return pltpu.make_async_remote_copy(
            src_ref=src,
            dst_ref=dst,
            send_sem=a2a_send.at[number, index],
            recv_sem=a2a_recv.at[number, index],
            device_id=peer(k),
            device_id_type=MESH,
        )

    total = pl.ds(0, (groups - 1) * HEAD)

    slab = rows.at[x]

    sent = []
    for side in range(2):
        cols = slice(side * middle, (side + 1) * middle)
        thin = slice(side * eighth, (side + 1) * eighth)
        number = 3 * side

        def dispatch(k, carry):
            to = at_group(lax.rem(me + k, groups))
            remote(number, 0, send_head.at[to, cols], slab.at[landing_group(me), cols], k).start()
            remote(number, 1, send_rest.at[to, thin], rest_in.at[at_group(me), thin], k).start()
            return carry

        lax.fori_loop(1, groups, dispatch, 0)
        sent.append(
            (
                remote(number, 0, send_head.at[total, cols], slab.at[total, cols], 1),
                remote(number, 1, send_rest.at[total, thin], rest_in.at[total, thin], 1),
            )
        )
    slab[landing_group(me), :] = send_head[at_group(me), :]
    rest_in[at_group(me), :] = send_rest[at_group(me), :]

    def send_back(number, part_of, src_head, src_rest, dst_head, dst_rest):
        def begin(i, carry):
            to = 2 * lax.rem(me // 2 + i, gh) + part_of

            @pl.when(to != me)
            def _():
                at = split_group(to)
                k = to - me + groups
                remote(number, 0, src_head.at[at, :], dst_head.at[at_group(me), :], k).start()
                remote(number, 1, src_rest.at[at, :], dst_rest.at[at_group(me), :], k).start()

            return carry

        lax.fori_loop(1, gh + 1, begin, 0)

        @pl.when(me % 2 == part_of)
        def _():
            dst_head[at_group(me), :] = src_head[split_group(me), :]
            dst_rest[at_group(me), :] = src_rest[split_group(me), :]

    def back(number, src_head, src_rest, dst_head, dst_rest):
        return (
            remote(number, 0, src_head.at[total, :], dst_head.at[total, :], 1),
            remote(number, 1, src_rest.at[total, :], dst_rest.at[total, :], 1),
        )

    for which, ref in (
        ((row_id % HEAD).astype(F32), mix_head),
        ((HEAD + row_id % REST).astype(F32), mix_rest),
    ):
        value = jnp.where(slot == which, share, 0.0).T
        high = value.astype(BF)
        ref[0:toks, :] = high
        ref[toks:, :] = (value - high.astype(F32)).astype(BF)

    loads[-1].wait()
    swaps[0].wait()
    for n in range(wide // lanes):
        cols = slice(n * lanes, (n + 1) * lanes)

        def down_peak(i, best):
            at = pl.ds(pl.multiple_of(i * 16, 16), 16)
            return jnp.maximum(best, jnp.abs(down[at, cols].astype(F32)))

        best = lax.fori_loop(0, hidden_all // 16, down_peak, jnp.zeros((16, lanes), F32))
        peak = jnp.max(best, axis=0, keepdims=True) + 1e-06
        col_mul[:, cols] = jnp.broadcast_to(7.0 / peak, (8, lanes))
        col_div[:, cols] = jnp.broadcast_to(peak / 7.0, (8, lanes))

        def down_level(i, carry):
            at = pl.ds(pl.multiple_of(i * 16, 16), 16)
            value = down[at, cols].astype(F32)
            mul = jnp.concatenate((col_mul[:, cols], col_mul[:, cols]), axis=0)
            down_q[at, cols] = soft_level(value * mul).astype(BF)
            return carry

        lax.fori_loop(0, hidden_all // 16, down_level, 0)

    for s in range(ring):
        loads[2 * s].wait()
        loads[2 * s + 1].wait()
        swaps[1 + 2 * s].wait()
        swaps[2 + 2 * s].wait()
        for n in range(wide // lanes):
            cols = slice(n * lanes, (n + 1) * lanes)

            def weight_top(i, best):
                at = pl.ds(pl.multiple_of(i * 16, 16), 16)
                return jnp.maximum(best, jnp.abs(weight[s, at, cols].astype(F32)))

            best = lax.fori_loop(0, 2 * hid2 // 16, weight_top, jnp.zeros((16, lanes), F32))
            peak_own[s, :, cols] = jnp.broadcast_to(jnp.max(best, axis=0, keepdims=True), (8, lanes))

    def small(number, k, src, dst):
        return pltpu.make_async_remote_copy(
            src_ref=src,
            dst_ref=dst,
            send_sem=small_send.at[number, k - 1],
            recv_sem=small_recv.at[number, k - 1],
            device_id=along(k),
            device_id_type=MESH,
        )

    peak_copies = [
        small(0, k, peak_own.at[lax.rem(x + k, ring)], peak_in.at[k - 1]) for k in range(1, ring)
    ]
    for copy in peak_copies:
        copy.start()
    for copy in peak_copies:
        copy.wait()
    weight_peak = peak_own[x]
    for k in range(1, ring):
        weight_peak = jnp.maximum(weight_peak, peak_in[k - 1])

    def ring_copy(number, ref, h, way, step, mag, to):
        if way == 0:
            owner = lax.rem(x - mag + ring, ring)
            part_of = step % 2
        else:
            owner = lax.rem(x + mag, ring)
            part_of = 1 - step % 2
        at = pl.ds(h * half + part_of * piece_rows, piece_rows)
        if ref is rows:
            piece = ref.at[owner, at, pl.ds((number // 3) * middle, middle)]
        else:
            piece = ref.at[owner, at, :]
        return pltpu.make_async_remote_copy(
            src_ref=piece,
            dst_ref=piece,
            send_sem=ring_send.at[number, h, way, step],
            recv_sem=ring_recv.at[number, h, way, step],
            device_id=along(to),
            device_id_type=MESH,
        )

    def hop(number, ref, h, way, step):
        return ring_copy(number, ref, h, way, step, step // 2, 1 if way == 0 else ring - 1)

    def landed(number, ref, h, way, step):
        return ring_copy(number, ref, h, way, step, 1 + step // 2, 1)

    def launch(number, ref, h, steps):
        for step in steps:
            for way in range(2):
                hop(number, ref, h, way, step).start()

    def await_step(number, ref, h, step):
        for way in range(2):
            landed(number, ref, h, way, step).wait_recv()

    def relay(number, ref, h):
        for way in range(2):
            landed(number, ref, h, way, 0).wait_recv()
            hop(number, ref, h, way, 2).start()

    def drain(number, ref):
        for h in range(2):
            for step in range(3):
                for way in range(2):
                    hop(number, ref, h, way, step).wait_send()

    pltpu.make_async_remote_copy(
        src_ref=top_send.at[pl.ds(0, (groups - 1) * tiles), :],
        dst_ref=top_in.at[pl.ds(0, (groups - 1) * tiles), :],
        send_sem=a2a_send.at[4, 0],
        recv_sem=a2a_recv.at[4, 0],
        device_id=peer(1),
        device_id_type=MESH,
    ).wait()
    act_peak = top_in[0:tiles, :]
    for g in range(1, groups):
        act_peak = jnp.maximum(act_peak, top_in[g * tiles : (g + 1) * tiles, :])
    act_peak = jnp.maximum(act_peak, 1.0)
    for n in range(tiles):
        cols = slice(n * 128, (n + 1) * 128)
        smooth[x, :, cols] = jnp.sqrt(act_peak[n : n + 1, :] / (weight_peak[:, cols] + 1e-06))
    smooth_copies = [small(1, k, smooth.at[x], smooth.at[x]) for k in range(1, ring)]
    for copy in smooth_copies:
        copy.start()
    for copy in smooth_copies:
        copy.wait()
    for s in range(ring):
        inv_smooth[s, :, :] = 1.0 / smooth[s]

    spread = iota((gh * REST, n_head), 1)
    home = iota((gh * REST, n_head), 0)

    def arrive(side):
        for copy in sent[side]:
            copy.wait_send()
            copy.wait_recv()
        for h in range(2):
            same_row = (spread // HEAD == 2 * (home // REST) + h) & (spread % REST == home % REST)
            for q in range(4):
                order = (same_row & ((spread // REST) % 4 == q)).astype(F32).astype(BF)
                slab[
                    h * half + half_head : (h + 1) * half,
                    side * middle + q * eighth : side * middle + (q + 1) * eighth,
                ] = dot_nn(order, rest_in[:, side * eighth : (side + 1) * eighth]).astype(BF)

    arrive(0)
    launch(0, rows, 0, (0, 1))

    def weight_level(i, carry):
        at = pl.ds(pl.multiple_of(i * 16, 16), 16)
        best = jnp.zeros((16, lanes), F32)
        for s in range(ring):
            for n in range(wide // lanes):
                cols = slice(n * lanes, (n + 1) * lanes)
                best = jnp.maximum(best, jnp.abs(weight[s, at, cols].astype(F32) * smooth[s, 0:1, cols]))
        peak = jnp.max(best, axis=1, keepdims=True) + 1e-06
        mul = 7.0 / peak
        div = peak / 7.0
        for s in range(ring):
            for n in range(wide // lanes):
                cols = slice(n * lanes, (n + 1) * lanes)
                value = weight[s, at, cols].astype(F32) * smooth[s, 0:1, cols]
                weight_q[s, at, cols] = (div * soft_level(value * mul)).astype(BF)
        return carry

    n_strip = 2 * hid2 // 16
    lax.fori_loop(0, n_strip // 2, weight_level, 0)
    relay(0, rows, 0)
    launch(0, rows, 1, (0,))
    lax.fori_loop(n_strip // 2, n_strip, weight_level, 0)

    arrive(1)
    eye = iota((block, block), 0) == iota((block, block), 1)
    top_rows = []
    for b in range(n_block):
        best = jnp.zeros((block, 128), F32)
        for n in range(tiles):
            cols = slice(n * 128, (n + 1) * 128)
            value = rows[x, b * block : (b + 1) * block, cols].astype(F32) * inv_smooth[x, 0:1, cols]
            best = jnp.maximum(best, jnp.abs(value))
        tall = jnp.max(best, axis=1, keepdims=True)
        top_rows.append(jnp.sum(jnp.where(eye, tall, 0.0), axis=0, keepdims=True))
    row_peak[x] = jnp.zeros((8, block), F32)
    for b in range(n_block):
        row_peak[x, b : b + 1, :] = top_rows[b]
    peak_rows = [small(2, k, row_peak.at[x], row_peak.at[x]) for k in range(1, ring)]
    for copy in peak_rows:
        copy.start()
    launch(3, rows, 0, (0, 1))

    strip = 16 if half % 16 == 0 else half

    def use_float(owner, h, first):
        at = pl.ds(h * half, half)
        product = dot_nt(rows[owner, at, :], weight[owner])
        acc_float[at, :] = product if first else acc_float[at, :] + product

    def use_quant(owner, h, first):
        at = pl.ds(h * half, half)

        def row_level(i, carry):
            here = pl.ds(h * half + i * strip, strip)
            out = pl.ds(i * strip, strip)
            mul = row_mul[here, 0:1]
            div = row_div[here, 0:1]
            for n in range(wide // lanes):
                cols = slice(n * lanes, (n + 1) * lanes)
                value = rows[owner, here, cols].astype(F32) * inv_smooth[owner, 0:1, cols]
                rows_q[out, cols] = (div * soft_level(value * mul)).astype(BF)
            return carry

        lax.fori_loop(0, half // strip, row_level, 0)
        product = dot_nt(rows_q[...], weight_q[owner])
        acc_quant[at, :] = product if first else acc_quant[at, :] + product

    def use_others(h):
        def one(i, carry):
            @pl.when(i == 0)
            def _():
                await_step(0, rows, h, 1)
                await_step(3, rows, h, 1)

            @pl.when(i == 2)
            def _():
                await_step(0, rows, h, 2)
                await_step(3, rows, h, 2)

            owner = lax.rem(x + ring - 1 + 2 * (i % 2) + 3 * (i // 2), ring)
            use_float(owner, h, False)
            use_quant(owner, h, False)
            return carry

        lax.fori_loop(0, ring - 1, one, 0)

    def activate(acc, out, h):
        def piece(i, carry):
            at = pl.ds(pl.multiple_of(h * half + i * strip, strip), strip)
            gate = acc[at, 0:hid2]
            up = acc[at, hid2:]
            out[x, at, :] = (gate / (1.0 + jnp.exp(-gate)) * up).astype(BF)
            return carry

        lax.fori_loop(0, half // strip, piece, 0)

    turn = iota((half_head, gh * REST), 0)
    base = iota((half_head, gh * REST), 1)
    back_row = (turn // HEAD == base // REST) & (turn % REST == base % REST)
    turn_part = (turn // REST) % 4

    def project(hidden, matrix, head, rest, h, scaled):
        rest_acc[...] = jnp.zeros_like(rest_acc)
        at = pl.ds(h * half, half)

        def piece(q, carry):
            cols = pl.ds(pl.multiple_of(q * quarter, quarter), quarter)
            total = dot_nn(hidden[0, at, :], matrix[0:hid2, cols])
            for s in range(1, ring):
                total = total + dot_nn(hidden[s, at, :], matrix[s * hid2 : (s + 1) * hid2, cols])
            if scaled:
                total = total * level_div[at, 0:1] * col_div[0:1, cols]
            total = total.astype(BF)
            head[h * half_head : (h + 1) * half_head, cols] = total[:half_head]
            order = (back_row & (turn_part == q)).astype(F32).astype(BF)
            rest_acc[...] += dot_nn(order, total[half_head:])
            return carry

        lax.fori_loop(0, 4, piece, 0)
        rest[h * half_head : (h + 1) * half_head, :] = rest_acc[...].astype(BF)

    def levels(h):
        def piece(i, carry):
            at = pl.ds(pl.multiple_of(h * half + i * strip, strip), strip)
            best = jnp.zeros((strip, hid2), F32)
            for s in range(ring):
                best = jnp.maximum(best, jnp.abs(hid_quant[s, at, :].astype(F32)))
            peak = jnp.max(best, axis=1, keepdims=True) + 1e-06
            mul = 7.0 / peak
            level_div[at, :] = jnp.broadcast_to(peak / 7.0, (strip, 128))
            for s in range(ring):
                hid_level[s, at, :] = soft_level(hid_quant[s, at, :].astype(F32) * mul).astype(BF)
            return carry

        lax.fori_loop(0, half // strip, piece, 0)

    use_float(x, 0, True)
    for copy in peak_rows:
        copy.wait()
    best_row = row_peak[0]
    for s in range(1, ring):
        best_row = jnp.maximum(best_row, row_peak[s])
    for b in range(n_block):
        flat = jnp.broadcast_to(best_row[b : b + 1, :], (block, block))
        tall = jnp.sum(jnp.where(eye, flat, 0.0), axis=1, keepdims=True) + 1e-06
        row_mul[b * block : (b + 1) * block, :] = jnp.broadcast_to(7.0 / tall, (block, 128))
        row_div[b * block : (b + 1) * block, :] = jnp.broadcast_to(tall / 7.0, (block, 128))
    use_quant(x, 0, True)
    relay(3, rows, 0)
    launch(0, rows, 1, (1,))
    relay(0, rows, 1)
    use_float(x, 1, True)
    launch(3, rows, 1, (0,))
    use_others(0)
    activate(acc_float, hid_float, 0)
    launch(1, hid_float, 0, (0, 1))
    activate(acc_quant, hid_quant, 0)
    launch(2, hid_quant, 0, (0, 1))
    use_quant(x, 1, True)
    relay(1, hid_float, 0)
    relay(2, hid_quant, 0)
    launch(3, rows, 1, (1,))
    relay(3, rows, 1)
    await_step(1, hid_float, 0, 1)
    await_step(1, hid_float, 0, 2)
    project(hid_float, down, outf_head, outf_rest, 0, False)
    send_back(1, 0, outf_head, outf_rest, backf_head, backf_rest)
    await_step(2, hid_quant, 0, 1)
    await_step(2, hid_quant, 0, 2)
    levels(0)
    project(hid_level, down_q, outq_head, outq_rest, 0, True)
    send_back(2, 0, outq_head, outq_rest, backq_head, backq_rest)
    use_others(1)
    activate(acc_float, hid_float, 1)
    launch(1, hid_float, 1, (0, 1))
    activate(acc_quant, hid_quant, 1)
    relay(1, hid_float, 1)
    launch(2, hid_quant, 1, (0, 1))
    await_step(1, hid_float, 1, 1)
    await_step(1, hid_float, 1, 2)
    project(hid_float, down, outf_head, outf_rest, 1, False)
    send_back(1, 1, outf_head, outf_rest, backf_head, backf_rest)
    relay(2, hid_quant, 1)
    await_step(2, hid_quant, 1, 1)
    await_step(2, hid_quant, 1, 2)
    levels(1)
    project(hid_level, down_q, outq_head, outq_rest, 1, True)
    send_back(2, 1, outq_head, outq_rest, backq_head, backq_rest)
    sent_float = back(1, outf_head, outf_rest, backf_head, backf_rest)
    sent_quant = back(2, outq_head, outq_rest, backq_head, backq_rest)

    def combine(number, head, rest):
        mixed = dot_nn(mix_head[...], head[...])
        mixed = mixed[:toks] + mixed[toks:]
        quarter_of = (iota((2 * toks, n_head), 1) // REST) % 4
        for q in range(4):
            weights = jnp.where(quarter_of == q, mix_rest[...].astype(F32), 0.0).astype(BF)
            extra = dot_nn(weights, rest[...])
            cols = slice(q * quarter, (q + 1) * quarter)
            first = (q * quarter) // width
            inner = q * quarter - first * width
            part[number, first, :, inner : inner + quarter] = mixed[:, cols] + extra[:toks] + extra[toks:]
        copy = pltpu.make_async_remote_copy(
            src_ref=part.at[number, 1 - core],
            dst_ref=part_in.at[number],
            send_sem=ex_send.at[number],
            recv_sem=ex_recv.at[number],
            device_id=partner,
            device_id_type=MESH,
        )
        copy.start()
        return copy

    for copy in sent_float:
        copy.wait_recv()
    half_float = combine(0, backf_head, backf_rest)
    half_float.wait()
    float_ref[...] = part[0, core] + part_in[0]
    for copy in sent_quant:
        copy.wait_recv()
    half_quant = combine(1, backq_head, backq_rest)

    for copy in sent_float:
        copy.wait_send()
    for copy in sent_quant:
        copy.wait_send()
    for number, ref in enumerate((rows, hid_float, hid_quant, rows)):
        drain(number, ref)
    half_quant.wait()
    quant_ref[...] = (part[1, core] + part_in[1]).astype(BF)


def solution(mesh):
    groups = mesh.shape["dp"]
    ring = mesh.shape["expert"] // 2

    def on_device(tokens, expert_ids, route_weights, gate_weight, up_weight, down_weight):
        toks, width = tokens.shape
        wide = 2 * width
        quarter = wide // 4
        hid = gate_weight.shape[1]
        hid2 = 2 * hid
        count = groups * CAP
        half = count // 2
        n_head = groups * HEAD
        hidden_all = ring * hid2
        block = 128 if count % 128 == 0 else count
        vmem = pltpu.VMEM
        dma = pltpu.SemaphoreType.DMA
        here = pl.BlockSpec(memory_space=pltpu.VMEM)
        away = pl.BlockSpec(memory_space=pl.ANY)
        return pl.pallas_call(
            functools.partial(layer_kernel, groups, ring),
            name="moe_layer",
            out_shape=(
                jax.ShapeDtypeStruct((toks, width), BF),
                jax.ShapeDtypeStruct((toks, width), F32),
            ),
            in_specs=[here, here, here, away, away, away],
            out_specs=(here, here),
            scratch_shapes=[
                vmem((toks, wide), BF),
                vmem((n_head, wide), BF),
                vmem((n_head, quarter), BF),
                vmem((ring, count, wide), BF),
                vmem((n_head, quarter), BF),
                vmem((ring, 2 * hid2, wide), BF),
                vmem((ring, 2 * hid2, wide), BF),
                vmem((hidden_all, wide), BF),
                vmem((hidden_all, wide), BF),
                vmem((half, wide), BF),
                vmem((count, 2 * hid2), F32),
                vmem((count, 2 * hid2), F32),
                vmem((ring, count, hid2), BF),
                vmem((ring, count, hid2), BF),
                vmem((ring, count, hid2), BF),
                vmem((ring, 8, wide), F32),
                vmem((ring - 1, 8, wide), F32),
                vmem((ring, 8, wide), F32),
                vmem((ring, 8, wide), F32),
                vmem((ring, 8, block), F32),
                vmem((count, 128), F32),
                vmem((count, 128), F32),
                vmem((count, 128), F32),
                vmem((8, wide), F32),
                vmem((8, wide), F32),
                vmem((groups * (wide // 128), 128), F32),
                vmem((groups * (wide // 128), 128), F32),
                vmem((2 * toks, n_head), BF),
                vmem((2 * toks, n_head), BF),
                vmem((n_head, wide), BF),
                vmem((n_head, quarter), BF),
                vmem((n_head, wide), BF),
                vmem((n_head, quarter), BF),
                vmem((n_head // 2, quarter), F32),
                vmem((n_head, wide), BF),
                vmem((n_head, quarter), BF),
                vmem((n_head, wide), BF),
                vmem((n_head, quarter), BF),
                vmem((2, 2, toks, width), F32),
                vmem((2, toks, width), F32),
                dma((2 * ring + 1,)),
                dma((2 + 2 * ring,)),
                dma((2 + 2 * ring,)),
                dma((5, 2)),
                dma((5, 2)),
                dma((3, ring - 1)),
                dma((3, ring - 1)),
                dma((4, 2, 2, 3)),
                dma((4, 2, 2, 3)),
                dma((2,)),
                dma((2,)),
            ],
            compiler_params=pltpu.CompilerParams(
                collective_id=0, has_side_effects=True, vmem_limit_bytes=64 * 1024 * 1024 - 128 * 1024
            ),
        )(
            tokens,
            expert_ids.T,
            route_weights.T,
            gate_weight,
            up_weight,
            down_weight,
        )

    in_specs = (
        P("dp", "expert"),
        P("dp", None),
        P("dp", None),
        P("dp", "expert", None),
        P("dp", "expert", None),
        P("dp", None, "expert"),
    )
    out_specs = (P("dp", "expert"), P("dp", "expert"))
    return jax.shard_map(
        on_device, mesh=mesh, in_specs=in_specs, out_specs=out_specs, check_vma=False
    )
```

```python
import functools

import jax
import jax.numpy as jnp
from jax import lax
from jax.experimental import pallas as pl
from jax.experimental.pallas import tpu as pltpu
from jax.sharding import PartitionSpec as P

MESH = pl.DeviceIdType.MESH
CAP = 20
HEAD = 16
REST = CAP - HEAD
BF = jnp.bfloat16
F32 = jnp.float32
COEF = (6.5788915972740805, -12.960054087409885, 11.90224462767755, -5.297839452865238)
ROUND = 12582912.0


def soft_level(values):
    whole = (values + ROUND) - ROUND
    rest = values - whole
    square = rest * rest
    poly = COEF[-1]
    for coef in COEF[-2::-1]:
        poly = poly * square + coef
    return whole + (rest * square) * poly


def dot_nt(a, b):
    return lax.dot_general(a, b, (((1,), (1,)), ((), ())), preferred_element_type=F32)


def dot_nn(a, b):
    return lax.dot_general(a, b, (((1,), (0,)), ((), ())), preferred_element_type=F32)


def iota(shape, axis):
    return lax.broadcasted_iota(jnp.int32, shape, axis)


def layer_kernel(
    groups,
    ring,
    tok_ref,
    ids_t_ref,
    route_ref,
    gate_hbm,
    up_hbm,
    down_hbm,
    both_ref,
    tok,
    send_head,
    send_rest,
    rows,
    rest_in,
    weight,
    weight_q,
    down,
    down_q,
    rows_q,
    rows_q2,
    acc_float,
    acc_quant,
    hid_float,
    hid_quant,
    hid_level,
    peak_own,
    peak_in,
    smooth,
    inv_smooth,
    row_peak,
    row_mul,
    row_div,
    level_div,
    col_mul,
    col_div,
    top_send,
    top_in,
    mix_head,
    mix_rest,
    outf_head,
    outf_rest,
    outq_head,
    outq_rest,
    rest_acc,
    backf_head,
    backf_rest,
    backq_head,
    backq_rest,
    part,
    part_in,
    tok_far,
    far_head,
    far_rest,
    far_in,
    tok_send,
    tok_recv,
    far_send,
    far_recv,
    load_sem,
    swap_send,
    swap_recv,
    a2a_send,
    a2a_recv,
    small_send,
    small_recv,
    ring_send,
    ring_recv,
    ex_send,
    ex_recv,
):
    me = lax.axis_index("dp")
    seat = lax.axis_index("expert")
    x = seat // 2
    core = seat % 2
    width = tok_ref.shape[1]
    wide = 2 * width
    quarter = wide // 4
    hid = gate_hbm.shape[1]
    hid2 = 2 * hid
    count = groups * CAP
    half = count // 2
    n_head = groups * HEAD
    gh = groups // 2
    half_head = gh * HEAD
    piece_rows = half // 2
    top = ids_t_ref.shape[0]
    toks = tok_ref.shape[0]
    lanes = min(512, wide)
    block = 128 if count % 128 == 0 else count
    n_block = count // block
    hidden_all = ring * hid2

    partner = (me, x * 2 + 1 - core)

    def along(k):
        return (me, lax.rem(x + k, ring) * 2 + core)

    def peer(k):
        return (lax.rem(me + k, groups), seat)

    loads = []
    for s in range(ring):
        for g, src in enumerate((gate_hbm, up_hbm)):
            loads.append(
                pltpu.make_async_copy(
                    src.at[core, :, pl.ds(s * wide, wide)],
                    weight.at[s, pl.ds(pl.multiple_of(g * hid2 + core * hid, 8), hid), :],
                    load_sem.at[2 * s + g],
                )
            )
    loads.append(
        pltpu.make_async_copy(
            down_hbm.at[core],
            down.at[:, pl.ds(pl.multiple_of(core * width, 128), width)],
            load_sem.at[2 * ring],
        )
    )
    loads[-1].start()
    for copy in loads[:-1]:
        copy.start()

    barrier = pltpu.get_barrier_semaphore()
    pl.semaphore_signal(barrier, inc=1, device_id=partner, device_id_type=MESH)
    for k in range(1, ring):
        pl.semaphore_signal(barrier, inc=1, device_id=along(k), device_id_type=MESH)

    def greet(k, carry):
        pl.semaphore_signal(barrier, inc=1, device_id=peer(k), device_id_type=MESH)
        return carry

    lax.fori_loop(1, groups, greet, 0)

    before = (iota((toks, toks), 0) < iota((toks, toks), 1)).astype(BF)
    row_id = iota((n_head, toks), 0)
    hit = jnp.zeros((n_head, toks), F32)
    wanted = (row_id // HEAD) * 2 + core
    share = jnp.zeros((n_head, toks), F32)
    ratio = route_ref[...]
    ratio = ratio / jnp.sum(ratio, axis=0, keepdims=True)
    for k in range(top):
        same = ids_t_ref[k : k + 1, :] == wanted
        hit = hit + same.astype(F32)
        share = share + jnp.where(same, ratio[k : k + 1, :], 0.0)
    slot = dot_nn(hit.astype(BF), before)
    pick_head = jnp.where(slot == (row_id % HEAD).astype(F32), hit, 0.0).astype(BF)
    pick_rest = jnp.where(slot == (HEAD + row_id % REST).astype(F32), hit, 0.0)
    part_id = (row_id // REST) % 4
    hit_group = jnp.zeros((groups, toks), F32)
    wanted = iota((groups, toks), 0) * 2 + core
    for k in range(top):
        hit_group = hit_group + (ids_t_ref[k : k + 1, :] == wanted).astype(F32)
    slot_group = dot_nn(hit_group.astype(BF), before)
    pick_all = jnp.concatenate(
        [jnp.where(slot_group == float(n), hit_group, 0.0).astype(BF) for n in range(CAP)], axis=0
    )
    tiles = wide // 128
    eighth = quarter // 2
    middle = wide // 2

    pl.semaphore_wait(barrier, 1 + (ring - 1) + (groups - 1))

    own_cols = pl.ds(pl.multiple_of(core * width, 128), width)
    tok_copy = pltpu.make_async_remote_copy(
        src_ref=tok_ref,
        dst_ref=tok.at[:, own_cols],
        send_sem=swap_send.at[0],
        recv_sem=swap_recv.at[0],
        device_id=partner,
        device_id_type=MESH,
    )
    tok_copy.start()
    tok[:, own_cols] = tok_ref[...]
    swaps = [
        pltpu.make_async_remote_copy(
            src_ref=down_hbm.at[1 - core],
            dst_ref=down.at[:, own_cols],
            send_sem=swap_send.at[1],
            recv_sem=swap_recv.at[1],
            device_id=partner,
            device_id_type=MESH,
        )
    ]
    for s in range(ring):
        for g, src in enumerate((gate_hbm, up_hbm)):
            swaps.append(
                pltpu.make_async_remote_copy(
                    src_ref=src.at[1 - core, :, pl.ds(s * wide, wide)],
                    dst_ref=weight.at[s, pl.ds(pl.multiple_of(g * hid2 + core * hid, 8), hid), :],
                    send_sem=swap_send.at[2 + 2 * s + g],
                    recv_sem=swap_recv.at[2 + 2 * s + g],
                    device_id=partner,
                    device_id_type=MESH,
                )
            )
    tok_copy.wait()
    odd = (me + me // 8) % 2 == 1

    def far_tokens(k):
        return pltpu.make_async_remote_copy(
            src_ref=tok.at[:, pl.ds(wide // 2, wide // 2)],
            dst_ref=tok_far.at[k - 1],
            send_sem=tok_send.at[k - 1],
            recv_sem=tok_recv.at[k - 1],
            device_id=along(k),
            device_id_type=MESH,
        )

    @pl.when(odd)
    def _():
        for k in range(1, ring):
            far_tokens(k).start()

    for copy in swaps:
        copy.start()

    every = jnp.abs(dot_nn(pick_all, tok[...]))
    highest = every[0:groups]
    for n in range(1, CAP):
        highest = jnp.maximum(highest, every[n * groups : (n + 1) * groups])
    for n in range(tiles):
        top_send[pl.ds(n, groups, stride=tiles), :] = highest[:, n * 128 : (n + 1) * 128]

    def top_at(g):
        return pl.ds(pl.multiple_of(g * tiles, tiles), tiles)

    def send_top(k, carry):
        pltpu.make_async_remote_copy(
            src_ref=top_send.at[top_at(lax.rem(me + k, groups)), :],
            dst_ref=top_in.at[top_at(me), :],
            send_sem=a2a_send.at[4, 0],
            recv_sem=a2a_recv.at[4, 0],
            device_id=peer(k),
            device_id_type=MESH,
        ).start()
        return carry

    lax.fori_loop(1, groups, send_top, 0)
    top_in[top_at(me), :] = top_send[top_at(me), :]

    send_head[...] = dot_nn(pick_head, tok[...]).astype(BF)
    chosen = jnp.zeros((n_head, quarter), F32)
    for q in range(4):
        pair = jnp.concatenate(
            (
                tok[:, q * eighth : (q + 1) * eighth],
                tok[:, middle + q * eighth : middle + (q + 1) * eighth],
            ),
            axis=1,
        )
        chosen = chosen + dot_nn(jnp.where(part_id == q, pick_rest, 0.0).astype(BF), pair)
    send_rest[...] = chosen.astype(BF)

    def side_of(g):
        return (g + g // 8) % 2

    def at_group(g):
        return pl.ds(pl.multiple_of(g * HEAD, HEAD), HEAD)

    def split_group(g):
        return pl.ds(pl.multiple_of(side_of(g) * half_head + (g // 2) * HEAD, HEAD), HEAD)

    def landing_group(g):
        return pl.ds(pl.multiple_of(side_of(g) * half + (g // 2) * HEAD, HEAD), HEAD)

    def remote(number, index, src, dst, k):
        return pltpu.make_async_remote_copy(
            src_ref=src,
            dst_ref=dst,
            send_sem=a2a_send.at[number, index],
            recv_sem=a2a_recv.at[number, index],
            device_id=peer(k),
            device_id_type=MESH,
        )

    total = pl.ds(0, (groups - 1) * HEAD)

    slab = rows.at[x]

    sent = []
    for side in range(2):
        cols = slice(side * middle, (side + 1) * middle)
        thin = slice(side * eighth, (side + 1) * eighth)
        number = 3 * side

        def dispatch(k, carry):
            to = at_group(lax.rem(me + k, groups))
            remote(number, 0, send_head.at[to, cols], slab.at[landing_group(me), cols], k).start()
            remote(number, 1, send_rest.at[to, thin], rest_in.at[at_group(me), thin], k).start()
            return carry

        lax.fori_loop(1, groups, dispatch, 0)
        sent.append(
            (
                remote(number, 0, send_head.at[total, cols], slab.at[total, cols], 1),
                remote(number, 1, send_rest.at[total, thin], rest_in.at[total, thin], 1),
            )
        )
    slab[landing_group(me), :] = send_head[at_group(me), :]
    rest_in[at_group(me), :] = send_rest[at_group(me), :]

    def send_back(number, part_of, src_head, src_rest, dst_head, dst_rest):
        def begin(i, carry):
            pair = lax.rem(me // 2 + i, gh)
            to = 2 * pair + (part_of + pair // 4) % 2

            @pl.when(to != me)
            def _():
                at = split_group(to)
                k = to - me + groups
                remote(number, 0, src_head.at[at, :], dst_head.at[at_group(me), :], k).start()
                remote(number, 1, src_rest.at[at, :], dst_rest.at[at_group(me), :], k).start()

            return carry

        lax.fori_loop(1, gh + 1, begin, 0)

        @pl.when(side_of(me) == part_of)
        def _():
            dst_head[at_group(me), :] = src_head[split_group(me), :]
            dst_rest[at_group(me), :] = src_rest[split_group(me), :]

    def back(number, src_head, src_rest, dst_head, dst_rest):
        return (
            remote(number, 0, src_head.at[total, :], dst_head.at[total, :], 1),
            remote(number, 1, src_rest.at[total, :], dst_rest.at[total, :], 1),
        )

    for which, ref in (
        ((row_id % HEAD).astype(F32), mix_head),
        ((HEAD + row_id % REST).astype(F32), mix_rest),
    ):
        value = jnp.where(slot == which, share, 0.0).T
        high = value.astype(BF)
        ref[0:toks, :] = high
        ref[toks:, :] = (value - high.astype(F32)).astype(BF)

    loads[-1].wait()
    swaps[0].wait()
    for n in range(wide // lanes):
        cols = slice(n * lanes, (n + 1) * lanes)

        def down_peak(i, best):
            at = pl.ds(pl.multiple_of(i * 16, 16), 16)
            return jnp.maximum(best, jnp.abs(down[at, cols].astype(F32)))

        best = lax.fori_loop(0, hidden_all // 16, down_peak, jnp.zeros((16, lanes), F32))
        peak = jnp.max(best, axis=0, keepdims=True) + 1e-06
        col_mul[:, cols] = jnp.broadcast_to(7.0 / peak, (8, lanes))
        col_div[:, cols] = jnp.broadcast_to(peak / 7.0, (8, lanes))

        def down_level(i, carry):
            at = pl.ds(pl.multiple_of(i * 16, 16), 16)
            value = down[at, cols].astype(F32)
            mul = jnp.concatenate((col_mul[:, cols], col_mul[:, cols]), axis=0)
            down_q[at, cols] = soft_level(value * mul).astype(BF)
            return carry

        lax.fori_loop(0, hidden_all // 16, down_level, 0)

    for s in range(ring):
        loads[2 * s].wait()
        loads[2 * s + 1].wait()
        swaps[1 + 2 * s].wait()
        swaps[2 + 2 * s].wait()
        for n in range(wide // lanes):
            cols = slice(n * lanes, (n + 1) * lanes)

            def weight_top(i, best):
                at = pl.ds(pl.multiple_of(i * 16, 16), 16)
                return jnp.maximum(best, jnp.abs(weight[s, at, cols].astype(F32)))

            best = lax.fori_loop(0, 2 * hid2 // 16, weight_top, jnp.zeros((16, lanes), F32))
            peak_own[s, :, cols] = jnp.broadcast_to(jnp.max(best, axis=0, keepdims=True), (8, lanes))

    def small(number, k, src, dst):
        return pltpu.make_async_remote_copy(
            src_ref=src,
            dst_ref=dst,
            send_sem=small_send.at[number, k - 1],
            recv_sem=small_recv.at[number, k - 1],
            device_id=along(k),
            device_id_type=MESH,
        )

    peak_copies = [
        small(0, k, peak_own.at[lax.rem(x + k, ring)], peak_in.at[k - 1]) for k in range(1, ring)
    ]
    for copy in peak_copies:
        copy.start()

    def far_copy(slot, src, dst, k):
        return pltpu.make_async_remote_copy(
            src_ref=src,
            dst_ref=dst,
            send_sem=far_send.at[slot],
            recv_sem=far_recv.at[slot],
            device_id=peer(k),
            device_id_type=MESH,
        )

    right_cols = slice(middle, wide)
    far_own = pl.ds(pl.multiple_of((me // 2) * HEAD, HEAD), HEAD)

    def far_owner(slot):
        return lax.rem(x + ring - 1 - slot, ring)

    @pl.when(odd)
    def _():
        for slot in range(ring - 1):
            far_tokens(slot + 1).wait()
            far_head[slot] = dot_nn(pick_head, tok_far[slot]).astype(BF)
            extra = jnp.zeros((n_head, eighth), F32)
            for q in range(4):
                extra = extra + dot_nn(
                    jnp.where(part_id == q, pick_rest, 0.0).astype(BF),
                    tok_far[slot, :, q * eighth : (q + 1) * eighth],
                )
            far_rest[:, slot * eighth : (slot + 1) * eighth] = extra.astype(BF)

        def far_dispatch(k, carry):
            to = at_group(lax.rem(me + k, groups))
            for slot in range(ring - 1):
                far_copy(
                    slot, far_head.at[slot, to, :], rows.at[far_owner(slot), landing_group(me), right_cols], k
                ).start()
            far_copy(ring - 1, far_rest.at[to, :], far_in.at[far_own, :], k).start()
            return carry

        lax.fori_loop(1, groups, far_dispatch, 0)
        for slot in range(ring - 1):
            rows[far_owner(slot), landing_group(me), right_cols] = far_head[slot, at_group(me), :]
        far_in[far_own, :] = far_rest[at_group(me), :]

    def far_arrive():
        for parity in range(min(2, gh)):

            @pl.when(side_of(me) == parity)
            def _():
                some = pl.ds(0, (gh - parity) * HEAD)
                for slot in range(ring - 1):
                    far_copy(slot, far_head.at[slot, some, :], rows.at[0, some, right_cols], 1).wait_recv()
                far_copy(ring - 1, far_rest.at[some, :], far_in.at[some, :], 1).wait_recv()

        near = iota((gh * REST, half_head), 1)
        base_row = iota((gh * REST, half_head), 0)
        same_row = (near // HEAD == base_row // REST) & (near % REST == base_row % REST)
        for q in range(4):
            order = (same_row & ((near // REST) % 4 == q)).astype(F32).astype(BF)
            moved = dot_nn(order, far_in[...]).astype(BF)
            for slot in range(ring - 1):
                rows[
                    far_owner(slot), half + half_head : 2 * half, middle + q * eighth : middle + (q + 1) * eighth
                ] = moved[:, slot * eighth : (slot + 1) * eighth]

    for copy in peak_copies:
        copy.wait()
    weight_peak = peak_own[x]
    for k in range(1, ring):
        weight_peak = jnp.maximum(weight_peak, peak_in[k - 1])

    def ring_copy(number, ref, h, way, step, mag, to):
        if way == 0:
            owner = lax.rem(x - mag + ring, ring)
            part_of = step % 2
        else:
            owner = lax.rem(x + mag, ring)
            part_of = 1 - step % 2
        at = pl.ds(h * half + part_of * piece_rows, piece_rows)
        if ref is rows:
            piece = ref.at[owner, at, pl.ds((number // 3) * middle, middle)]
        else:
            piece = ref.at[owner, at, :]
        return pltpu.make_async_remote_copy(
            src_ref=piece,
            dst_ref=piece,
            send_sem=ring_send.at[number, h, way, step],
            recv_sem=ring_recv.at[number, h, way, step],
            device_id=along(to),
            device_id_type=MESH,
        )

    def hop(number, ref, h, way, step):
        return ring_copy(number, ref, h, way, step, step // 2, 1 if way == 0 else ring - 1)

    def landed(number, ref, h, way, step):
        return ring_copy(number, ref, h, way, step, 1 + step // 2, 1)

    def launch(number, ref, h, steps):
        for step in steps:
            for way in range(2):
                hop(number, ref, h, way, step).start()

    def await_step(number, ref, h, step):
        for way in range(2):
            landed(number, ref, h, way, step).wait_recv()

    def relay(number, ref, h):
        for way in range(2):
            landed(number, ref, h, way, 0).wait_recv()
            hop(number, ref, h, way, 2).start()

    def drain(number, ref):
        for h in range(1 if number == 3 else 2):
            for step in range(3):
                for way in range(2):
                    hop(number, ref, h, way, step).wait_send()

    pltpu.make_async_remote_copy(
        src_ref=top_send.at[pl.ds(0, (groups - 1) * tiles), :],
        dst_ref=top_in.at[pl.ds(0, (groups - 1) * tiles), :],
        send_sem=a2a_send.at[4, 0],
        recv_sem=a2a_recv.at[4, 0],
        device_id=peer(1),
        device_id_type=MESH,
    ).wait()
    act_peak = top_in[0:tiles, :]
    for g in range(1, groups):
        act_peak = jnp.maximum(act_peak, top_in[g * tiles : (g + 1) * tiles, :])
    act_peak = jnp.maximum(act_peak, 1.0)
    for n in range(tiles):
        cols = slice(n * 128, (n + 1) * 128)
        smooth[x, :, cols] = jnp.sqrt(act_peak[n : n + 1, :] / (weight_peak[:, cols] + 1e-06))
    smooth_copies = [small(1, k, smooth.at[x], smooth.at[x]) for k in range(1, ring)]
    for copy in smooth_copies:
        copy.start()
    for copy in smooth_copies:
        copy.wait()
    for s in range(ring):
        inv_smooth[s, :, :] = 1.0 / smooth[s]

    spread = iota((gh * REST, n_head), 1)
    home = iota((gh * REST, n_head), 0)

    def arrive(side):
        for copy in sent[side]:
            copy.wait_send()
            copy.wait_recv()
        for h in range(2):
            same_row = (spread // HEAD == 2 * (home // REST) + (h + home // (4 * REST)) % 2) & (spread % REST == home % REST)
            for q in range(4):
                order = (same_row & ((spread // REST) % 4 == q)).astype(F32).astype(BF)
                slab[
                    h * half + half_head : (h + 1) * half,
                    side * middle + q * eighth : side * middle + (q + 1) * eighth,
                ] = dot_nn(order, rest_in[:, side * eighth : (side + 1) * eighth]).astype(BF)

    arrive(0)
    launch(0, rows, 0, (0, 1))

    def weight_level(i, carry):
        at = pl.ds(pl.multiple_of(i * 16, 16), 16)
        best = jnp.zeros((16, lanes), F32)
        for s in range(ring):
            for n in range(wide // lanes):
                cols = slice(n * lanes, (n + 1) * lanes)
                best = jnp.maximum(best, jnp.abs(weight[s, at, cols].astype(F32) * smooth[s, 0:1, cols]))
        peak = jnp.max(best, axis=1, keepdims=True) + 1e-06
        mul = 7.0 / peak
        div = peak / 7.0
        for s in range(ring):
            for n in range(wide // lanes):
                cols = slice(n * lanes, (n + 1) * lanes)
                value = weight[s, at, cols].astype(F32) * smooth[s, 0:1, cols]
                weight_q[s, at, cols] = (div * soft_level(value * mul)).astype(BF)
        return carry

    n_strip = 2 * hid2 // 16
    lax.fori_loop(0, n_strip // 2, weight_level, 0)
    relay(0, rows, 0)
    launch(0, rows, 1, (0,))
    lax.fori_loop(n_strip // 2, n_strip, weight_level, 0)

    arrive(1)
    eye = iota((block, block), 0) == iota((block, block), 1)
    top_rows = []
    for b in range(n_block):
        best = jnp.zeros((block, 128), F32)
        for n in range(tiles):
            cols = slice(n * 128, (n + 1) * 128)
            value = rows[x, b * block : (b + 1) * block, cols].astype(F32) * inv_smooth[x, 0:1, cols]
            best = jnp.maximum(best, jnp.abs(value))
        tall = jnp.max(best, axis=1, keepdims=True)
        top_rows.append(jnp.sum(jnp.where(eye, tall, 0.0), axis=0, keepdims=True))
    row_peak[x] = jnp.zeros((8, block), F32)
    for b in range(n_block):
        row_peak[x, b : b + 1, :] = top_rows[b]
    peak_rows = [small(2, k, row_peak.at[x], row_peak.at[x]) for k in range(1, ring)]
    for copy in peak_rows:
        copy.start()
    launch(3, rows, 0, (0, 1))

    strip = 16 if half % 16 == 0 else half

    def use_float(owner, h, first):
        at = pl.ds(h * half, half)
        product = dot_nt(rows[owner, at, :], weight[owner])
        acc_float[at, :] = product if first else acc_float[at, :] + product

    def level_rows(owner, h, out):
        for i in range(half // strip):
            here = slice(h * half + i * strip, h * half + (i + 1) * strip)
            mul = row_mul[here, 0:1]
            div = row_div[here, 0:1]
            for n in range(wide // lanes):
                cols = slice(n * lanes, (n + 1) * lanes)
                value = rows[owner, here, cols].astype(F32) * inv_smooth[owner, 0:1, cols]
                out[i * strip : (i + 1) * strip, cols] = (div * soft_level(value * mul)).astype(BF)

    def use_quant(owner, h, first, buf):
        at = pl.ds(h * half, half)
        product = dot_nt(buf[...], weight_q[owner])
        acc_quant[at, :] = product if first else acc_quant[at, :] + product

    def use_others(h):
        left = lax.rem(x + ring - 1, ring)
        right = lax.rem(x + 1, ring)
        across = lax.rem(x + 2, ring)
        await_step(0, rows, h, 1)
        if h == 0:
            await_step(3, rows, h, 1)
        use_float(left, h, False)
        level_rows(left, h, rows_q)
        use_float(right, h, False)
        level_rows(right, h, rows_q2)
        use_quant(left, h, False, rows_q)
        use_quant(right, h, False, rows_q2)
        await_step(0, rows, h, 2)
        if h == 0:
            await_step(3, rows, h, 2)
        use_float(across, h, False)
        level_rows(across, h, rows_q)
        use_quant(across, h, False, rows_q)

    def activate(acc, out, h):
        def piece(i, carry):
            at = pl.ds(pl.multiple_of(h * half + i * strip, strip), strip)
            gate = acc[at, 0:hid2]
            up = acc[at, hid2:]
            out[x, at, :] = (gate / (1.0 + jnp.exp(-gate)) * up).astype(BF)
            return carry

        lax.fori_loop(0, half // strip, piece, 0)

    turn = iota((half_head, gh * REST), 0)
    base = iota((half_head, gh * REST), 1)
    back_row = (turn // HEAD == base // REST) & (turn % REST == base % REST)
    turn_part = (turn // REST) % 4

    def project(hidden, matrix, head, rest, h, scaled):
        rest_acc[...] = jnp.zeros_like(rest_acc)
        at = pl.ds(h * half, half)

        def piece(q, carry):
            cols = pl.ds(pl.multiple_of(q * quarter, quarter), quarter)
            total = dot_nn(hidden[0, at, :], matrix[0:hid2, cols])
            for s in range(1, ring):
                total = total + dot_nn(hidden[s, at, :], matrix[s * hid2 : (s + 1) * hid2, cols])
            if scaled:
                total = total * level_div[at, 0:1] * col_div[0:1, cols]
            total = total.astype(BF)
            head[h * half_head : (h + 1) * half_head, cols] = total[:half_head]
            order = (back_row & (turn_part == q)).astype(F32).astype(BF)
            rest_acc[...] += dot_nn(order, total[half_head:])
            return carry

        lax.fori_loop(0, 4, piece, 0)
        rest[h * half_head : (h + 1) * half_head, :] = rest_acc[...].astype(BF)

    def levels(h):
        def piece(i, carry):
            at = pl.ds(pl.multiple_of(h * half + i * strip, strip), strip)
            best = jnp.zeros((strip, hid2), F32)
            for s in range(ring):
                best = jnp.maximum(best, jnp.abs(hid_quant[s, at, :].astype(F32)))
            peak = jnp.max(best, axis=1, keepdims=True) + 1e-06
            mul = 7.0 / peak
            level_div[at, :] = jnp.broadcast_to(peak / 7.0, (strip, 128))
            for s in range(ring):
                hid_level[s, at, :] = soft_level(hid_quant[s, at, :].astype(F32) * mul).astype(BF)
            return carry

        lax.fori_loop(0, half // strip, piece, 0)

    use_float(x, 0, True)
    use_float(x, 1, True)
    for copy in peak_rows:
        copy.wait()
    best_row = row_peak[0]
    for s in range(1, ring):
        best_row = jnp.maximum(best_row, row_peak[s])
    for b in range(n_block):
        flat = jnp.broadcast_to(best_row[b : b + 1, :], (block, block))
        tall = jnp.sum(jnp.where(eye, flat, 0.0), axis=1, keepdims=True) + 1e-06
        row_mul[b * block : (b + 1) * block, :] = jnp.broadcast_to(7.0 / tall, (block, 128))
        row_div[b * block : (b + 1) * block, :] = jnp.broadcast_to(tall / 7.0, (block, 128))
    level_rows(x, 0, rows_q)
    use_quant(x, 0, True, rows_q)
    relay(3, rows, 0)
    launch(0, rows, 1, (1,))
    use_others(0)
    activate(acc_float, hid_float, 0)
    launch(1, hid_float, 0, (0, 1))
    activate(acc_quant, hid_quant, 0)
    level_rows(x, 1, rows_q)
    use_quant(x, 1, True, rows_q)
    relay(1, hid_float, 0)
    launch(2, hid_quant, 0, (0, 1))
    relay(0, rows, 1)
    await_step(1, hid_float, 0, 1)
    await_step(1, hid_float, 0, 2)
    project(hid_float, down, outf_head, outf_rest, 0, False)
    send_back(1, 0, outf_head, outf_rest, backf_head, backf_rest)
    relay(2, hid_quant, 0)
    await_step(2, hid_quant, 0, 1)
    await_step(2, hid_quant, 0, 2)
    levels(0)
    project(hid_level, down_q, outq_head, outq_rest, 0, True)
    send_back(2, 0, outq_head, outq_rest, backq_head, backq_rest)
    far_arrive()
    use_others(1)
    activate(acc_float, hid_float, 1)
    launch(1, hid_float, 1, (0, 1))
    activate(acc_quant, hid_quant, 1)
    relay(1, hid_float, 1)
    launch(2, hid_quant, 1, (0, 1))
    await_step(1, hid_float, 1, 1)
    await_step(1, hid_float, 1, 2)
    project(hid_float, down, outf_head, outf_rest, 1, False)
    send_back(1, 1, outf_head, outf_rest, backf_head, backf_rest)
    relay(2, hid_quant, 1)
    await_step(2, hid_quant, 1, 1)
    await_step(2, hid_quant, 1, 2)
    levels(1)
    project(hid_level, down_q, outq_head, outq_rest, 1, True)
    send_back(2, 1, outq_head, outq_rest, backq_head, backq_rest)
    sent_float = back(1, outf_head, outf_rest, backf_head, backf_rest)
    sent_quant = back(2, outq_head, outq_rest, backq_head, backq_rest)

    def combine(number, head, rest):
        mixed = dot_nn(mix_head[...], head[...])
        mixed = mixed[:toks] + mixed[toks:]
        quarter_of = (iota((2 * toks, n_head), 1) // REST) % 4
        for q in range(4):
            weights = jnp.where(quarter_of == q, mix_rest[...].astype(F32), 0.0).astype(BF)
            extra = dot_nn(weights, rest[...])
            cols = slice(q * quarter, (q + 1) * quarter)
            first = (q * quarter) // width
            inner = q * quarter - first * width
            part[number, first, :, inner : inner + quarter] = mixed[:, cols] + extra[:toks] + extra[toks:]
        copy = pltpu.make_async_remote_copy(
            src_ref=part.at[number, 1 - core],
            dst_ref=part_in.at[number],
            send_sem=ex_send.at[number],
            recv_sem=ex_recv.at[number],
            device_id=partner,
            device_id_type=MESH,
        )
        copy.start()
        return copy

    for copy in sent_float:
        copy.wait_recv()
    half_float = combine(0, backf_head, backf_rest)
    half_float.wait()
    both_ref[0] = part[0, core] + part_in[0]
    for copy in sent_quant:
        copy.wait_recv()
    half_quant = combine(1, backq_head, backq_rest)

    for copy in sent_float:
        copy.wait_send()
    for copy in sent_quant:
        copy.wait_send()

    @pl.when(odd)
    def _():
        for slot in range(ring - 1):
            far_copy(slot, far_head.at[slot, total, :], far_head.at[slot, total, :], 1).wait_send()
        far_copy(ring - 1, far_rest.at[total, :], far_rest.at[total, :], 1).wait_send()

    for number, ref in enumerate((rows, hid_float, hid_quant, rows)):
        drain(number, ref)
    half_quant.wait()
    both_ref[1] = part[1, core] + part_in[1]


def solution(mesh):
    groups = mesh.shape["dp"]
    ring = mesh.shape["expert"] // 2

    def on_device(tokens, expert_ids, route_weights, gate_weight, up_weight, down_weight):
        toks, width = tokens.shape
        wide = 2 * width
        quarter = wide // 4
        hid = gate_weight.shape[1]
        hid2 = 2 * hid
        count = groups * CAP
        half = count // 2
        n_head = groups * HEAD
        hidden_all = ring * hid2
        block = 128 if count % 128 == 0 else count
        vmem = pltpu.VMEM
        dma = pltpu.SemaphoreType.DMA
        here = pl.BlockSpec(memory_space=pltpu.VMEM)
        away = pl.BlockSpec(memory_space=pl.ANY)
        both = pl.pallas_call(
            functools.partial(layer_kernel, groups, ring),
            name="moe_layer",
            out_shape=jax.ShapeDtypeStruct((2, toks, width), F32),
            in_specs=[here, here, here, away, away, away],
            out_specs=here,
            scratch_shapes=[
                vmem((toks, wide), BF),
                vmem((n_head, wide), BF),
                vmem((n_head, quarter), BF),
                vmem((ring, count, wide), BF),
                vmem((n_head, quarter), BF),
                vmem((ring, 2 * hid2, wide), BF),
                vmem((ring, 2 * hid2, wide), BF),
                vmem((hidden_all, wide), BF),
                vmem((hidden_all, wide), BF),
                vmem((half, wide), BF),
                vmem((half, wide), BF),
                vmem((count, 2 * hid2), F32),
                vmem((count, 2 * hid2), F32),
                vmem((ring, count, hid2), BF),
                vmem((ring, count, hid2), BF),
                vmem((ring, count, hid2), BF),
                vmem((ring, 8, wide), F32),
                vmem((ring - 1, 8, wide), F32),
                vmem((ring, 8, wide), F32),
                vmem((ring, 8, wide), F32),
                vmem((ring, 8, block), F32),
                vmem((count, 128), F32),
                vmem((count, 128), F32),
                vmem((count, 128), F32),
                vmem((8, wide), F32),
                vmem((8, wide), F32),
                vmem((groups * (wide // 128), 128), F32),
                vmem((groups * (wide // 128), 128), F32),
                vmem((2 * toks, n_head), BF),
                vmem((2 * toks, n_head), BF),
                vmem((n_head, wide), BF),
                vmem((n_head, quarter), BF),
                vmem((n_head, wide), BF),
                vmem((n_head, quarter), BF),
                vmem((n_head // 2, quarter), F32),
                vmem((n_head, wide), BF),
                vmem((n_head, quarter), BF),
                vmem((n_head, wide), BF),
                vmem((n_head, quarter), BF),
                vmem((2, 2, toks, width), F32),
                vmem((2, toks, width), F32),
                vmem((ring - 1, toks, wide // 2), BF),
                vmem((ring - 1, n_head, wide // 2), BF),
                vmem((n_head, (ring - 1) * quarter // 2), BF),
                vmem((n_head // 2, (ring - 1) * quarter // 2), BF),
                dma((ring - 1,)),
                dma((ring - 1,)),
                dma((ring,)),
                dma((ring,)),
                dma((2 * ring + 1,)),
                dma((2 + 2 * ring,)),
                dma((2 + 2 * ring,)),
                dma((5, 2)),
                dma((5, 2)),
                dma((3, ring - 1)),
                dma((3, ring - 1)),
                dma((4, 2, 2, 3)),
                dma((4, 2, 2, 3)),
                dma((2,)),
                dma((2,)),
            ],
            compiler_params=pltpu.CompilerParams(
                collective_id=0, has_side_effects=True, vmem_limit_bytes=64 * 1024 * 1024 - 128 * 1024
            ),
        )(
            tokens,
            expert_ids.T,
            route_weights.T,
            gate_weight,
            up_weight,
            down_weight,
        )
        return both[1].astype(BF), both[0]

    in_specs = (
        P("dp", "expert"),
        P("dp", None),
        P("dp", None),
        P("dp", "expert", None),
        P("dp", "expert", None),
        P("dp", None, "expert"),
    )
    out_specs = (P("dp", "expert"), P("dp", "expert"))
    return jax.shard_map(
        on_device, mesh=mesh, in_specs=in_specs, out_specs=out_specs, check_vma=False
    )
```

```python
import functools

import jax
import jax.numpy as jnp
from jax import lax
from jax.experimental import pallas as pl
from jax.experimental.pallas import tpu as pltpu
from jax.sharding import PartitionSpec as P

MESH = pl.DeviceIdType.MESH
CAP = 20
HEAD = 16
REST = CAP - HEAD
BF = jnp.bfloat16
F32 = jnp.float32
COEF = (6.5788915972740805, -12.960054087409885, 11.90224462767755, -5.297839452865238)
ROUND = 12582912.0


def soft_level(values):
    whole = (values + ROUND) - ROUND
    rest = values - whole
    square = rest * rest
    poly = COEF[-1]
    for coef in COEF[-2::-1]:
        poly = poly * square + coef
    return whole + (rest * square) * poly


def dot_nt(a, b):
    return lax.dot_general(a, b, (((1,), (1,)), ((), ())), preferred_element_type=F32)


def dot_nn(a, b):
    return lax.dot_general(a, b, (((1,), (0,)), ((), ())), preferred_element_type=F32)


def iota(shape, axis):
    return lax.broadcasted_iota(jnp.int32, shape, axis)


def layer_kernel(
    groups,
    ring,
    tok_ref,
    ids_t_ref,
    route_ref,
    gate_hbm,
    up_hbm,
    down_hbm,
    both_ref,
    tok,
    send_head,
    send_rest,
    rows,
    rest_in,
    weight,
    weight_q,
    down,
    down_q,
    rows_q,
    rows_q2,
    acc_float,
    acc_quant,
    hid_float,
    hid_quant,
    hid_level,
    peak_own,
    peak_in,
    smooth,
    inv_smooth,
    row_peak,
    row_mul,
    row_div,
    level_div,
    col_mul,
    col_div,
    top_send,
    top_in,
    mix_head,
    mix_rest,
    outf_head,
    outf_rest,
    outq_head,
    outq_rest,
    rest_acc,
    backf_head,
    backf_rest,
    backq_head,
    backq_rest,
    part,
    part_in,
    tok_far,
    far_head,
    far_rest,
    far_in,
    tok_send,
    tok_recv,
    far_send,
    far_recv,
    load_sem,
    swap_send,
    swap_recv,
    a2a_send,
    a2a_recv,
    small_send,
    small_recv,
    ring_send,
    ring_recv,
    ex_send,
    ex_recv,
):
    me = lax.axis_index("dp")
    seat = lax.axis_index("expert")
    x = seat // 2
    core = seat % 2
    width = tok_ref.shape[1]
    wide = 2 * width
    quarter = wide // 4
    hid = gate_hbm.shape[1]
    hid2 = 2 * hid
    count = groups * CAP
    half = count // 2
    n_head = groups * HEAD
    gh = groups // 2
    half_head = gh * HEAD
    piece_rows = half // 2
    top = ids_t_ref.shape[0]
    toks = tok_ref.shape[0]
    lanes = min(512, wide)
    block = 128 if count % 128 == 0 else count
    n_block = count // block
    hidden_all = ring * hid2

    partner = (me, x * 2 + 1 - core)

    def along(k):
        return (me, lax.rem(x + k, ring) * 2 + core)

    def peer(k):
        return (lax.rem(me + k, groups), seat)

    loads = []
    for s in range(ring):
        for g, src in enumerate((gate_hbm, up_hbm)):
            loads.append(
                pltpu.make_async_copy(
                    src.at[core, :, pl.ds(s * wide, wide)],
                    weight.at[s, pl.ds(pl.multiple_of(g * hid2 + core * hid, 8), hid), :],
                    load_sem.at[2 * s + g],
                )
            )
    loads.append(
        pltpu.make_async_copy(
            down_hbm.at[core],
            down.at[:, pl.ds(pl.multiple_of(core * width, 128), width)],
            load_sem.at[2 * ring],
        )
    )
    loads[-1].start()
    for copy in loads[:-1]:
        copy.start()

    barrier = pltpu.get_barrier_semaphore()
    pl.semaphore_signal(barrier, inc=1, device_id=partner, device_id_type=MESH)
    for k in range(1, ring):
        pl.semaphore_signal(barrier, inc=1, device_id=along(k), device_id_type=MESH)

    def greet(k, carry):
        pl.semaphore_signal(barrier, inc=1, device_id=peer(k), device_id_type=MESH)
        return carry

    lax.fori_loop(1, groups, greet, 0)

    before = (iota((toks, toks), 0) < iota((toks, toks), 1)).astype(BF)
    row_id = iota((n_head, toks), 0)
    hit = jnp.zeros((n_head, toks), F32)
    wanted = (row_id // HEAD) * 2 + core
    share = jnp.zeros((n_head, toks), F32)
    ratio = route_ref[...]
    ratio = ratio / jnp.sum(ratio, axis=0, keepdims=True)
    for k in range(top):
        same = ids_t_ref[k : k + 1, :] == wanted
        hit = hit + same.astype(F32)
        share = share + jnp.where(same, ratio[k : k + 1, :], 0.0)
    slot = dot_nn(hit.astype(BF), before)
    pick_head = jnp.where(slot == (row_id % HEAD).astype(F32), hit, 0.0).astype(BF)
    pick_rest = jnp.where(slot == (HEAD + row_id % REST).astype(F32), hit, 0.0)
    part_id = (row_id // REST) % 4
    hit_group = jnp.zeros((groups, toks), F32)
    wanted = iota((groups, toks), 0) * 2 + core
    for k in range(top):
        hit_group = hit_group + (ids_t_ref[k : k + 1, :] == wanted).astype(F32)
    slot_group = dot_nn(hit_group.astype(BF), before)
    pick_all = jnp.concatenate(
        [jnp.where(slot_group == float(n), hit_group, 0.0).astype(BF) for n in range(CAP)], axis=0
    )
    tiles = wide // 128
    eighth = quarter // 2
    middle = wide // 2

    pl.semaphore_wait(barrier, 1 + (ring - 1) + (groups - 1))

    own_cols = pl.ds(pl.multiple_of(core * width, 128), width)
    tok_copy = pltpu.make_async_remote_copy(
        src_ref=tok_ref,
        dst_ref=tok.at[:, own_cols],
        send_sem=swap_send.at[0],
        recv_sem=swap_recv.at[0],
        device_id=partner,
        device_id_type=MESH,
    )
    tok_copy.start()
    tok[:, own_cols] = tok_ref[...]
    swaps = [
        pltpu.make_async_remote_copy(
            src_ref=down_hbm.at[1 - core],
            dst_ref=down.at[:, own_cols],
            send_sem=swap_send.at[1],
            recv_sem=swap_recv.at[1],
            device_id=partner,
            device_id_type=MESH,
        )
    ]
    for s in range(ring):
        for g, src in enumerate((gate_hbm, up_hbm)):
            swaps.append(
                pltpu.make_async_remote_copy(
                    src_ref=src.at[1 - core, :, pl.ds(s * wide, wide)],
                    dst_ref=weight.at[s, pl.ds(pl.multiple_of(g * hid2 + core * hid, 8), hid), :],
                    send_sem=swap_send.at[2 + 2 * s + g],
                    recv_sem=swap_recv.at[2 + 2 * s + g],
                    device_id=partner,
                    device_id_type=MESH,
                )
            )
    tok_copy.wait()
    odd = (me + me // 8) % 2 == 1

    def far_tokens(k):
        return pltpu.make_async_remote_copy(
            src_ref=tok.at[:, pl.ds(wide // 2, wide // 2)],
            dst_ref=tok_far.at[k - 1],
            send_sem=tok_send.at[k - 1],
            recv_sem=tok_recv.at[k - 1],
            device_id=along(k),
            device_id_type=MESH,
        )

    @pl.when(odd)
    def _():
        for k in range(1, ring):
            far_tokens(k).start()

    for copy in swaps:
        copy.start()

    every = jnp.abs(dot_nn(pick_all, tok[...]))
    highest = every[0:groups]
    for n in range(1, CAP):
        highest = jnp.maximum(highest, every[n * groups : (n + 1) * groups])
    for n in range(tiles):
        top_send[pl.ds(n, groups, stride=tiles), :] = highest[:, n * 128 : (n + 1) * 128]

    def top_at(g):
        return pl.ds(pl.multiple_of(g * tiles, tiles), tiles)

    def send_top(k, carry):
        pltpu.make_async_remote_copy(
            src_ref=top_send.at[top_at(lax.rem(me + k, groups)), :],
            dst_ref=top_in.at[top_at(me), :],
            send_sem=a2a_send.at[4, 0],
            recv_sem=a2a_recv.at[4, 0],
            device_id=peer(k),
            device_id_type=MESH,
        ).start()
        return carry

    lax.fori_loop(1, groups, send_top, 0)
    top_in[top_at(me), :] = top_send[top_at(me), :]

    send_head[...] = dot_nn(pick_head, tok[...]).astype(BF)
    chosen = jnp.zeros((n_head, quarter), F32)
    for q in range(4):
        pair = jnp.concatenate(
            (
                tok[:, q * eighth : (q + 1) * eighth],
                tok[:, middle + q * eighth : middle + (q + 1) * eighth],
            ),
            axis=1,
        )
        chosen = chosen + dot_nn(jnp.where(part_id == q, pick_rest, 0.0).astype(BF), pair)
    send_rest[...] = chosen.astype(BF)

    def side_of(g):
        return (g + g // 8) % 2

    def at_group(g):
        return pl.ds(pl.multiple_of(g * HEAD, HEAD), HEAD)

    def split_group(g):
        return pl.ds(pl.multiple_of(side_of(g) * half_head + (g // 2) * HEAD, HEAD), HEAD)

    def landing_group(g):
        return pl.ds(pl.multiple_of(side_of(g) * half + (g // 2) * HEAD, HEAD), HEAD)

    def remote(number, index, src, dst, k):
        return pltpu.make_async_remote_copy(
            src_ref=src,
            dst_ref=dst,
            send_sem=a2a_send.at[number, index],
            recv_sem=a2a_recv.at[number, index],
            device_id=peer(k),
            device_id_type=MESH,
        )

    total = pl.ds(0, (groups - 1) * HEAD)

    slab = rows.at[x]

    sent = []
    for side in range(2):
        cols = slice(side * middle, (side + 1) * middle)
        thin = slice(side * eighth, (side + 1) * eighth)
        number = 3 * side

        def dispatch(k, carry):
            to = at_group(lax.rem(me + k, groups))
            remote(number, 0, send_head.at[to, cols], slab.at[landing_group(me), cols], k).start()
            remote(number, 1, send_rest.at[to, thin], rest_in.at[at_group(me), thin], k).start()
            return carry

        lax.fori_loop(1, groups, dispatch, 0)
        sent.append(
            (
                remote(number, 0, send_head.at[total, cols], slab.at[total, cols], 1),
                remote(number, 1, send_rest.at[total, thin], rest_in.at[total, thin], 1),
            )
        )
    slab[landing_group(me), :] = send_head[at_group(me), :]
    rest_in[at_group(me), :] = send_rest[at_group(me), :]

    def send_back(number, part_of, src_head, src_rest, dst_head, dst_rest):
        def begin(i, carry):
            pair = lax.rem(me // 2 + i, gh)
            to = 2 * pair + (part_of + pair // 4) % 2

            @pl.when(to != me)
            def _():
                at = split_group(to)
                k = to - me + groups
                remote(number, 0, src_head.at[at, :], dst_head.at[at_group(me), :], k).start()
                remote(number, 1, src_rest.at[at, :], dst_rest.at[at_group(me), :], k).start()

            return carry

        lax.fori_loop(1, gh + 1, begin, 0)

        @pl.when(side_of(me) == part_of)
        def _():
            dst_head[at_group(me), :] = src_head[split_group(me), :]
            dst_rest[at_group(me), :] = src_rest[split_group(me), :]

    def back(number, src_head, src_rest, dst_head, dst_rest):
        return (
            remote(number, 0, src_head.at[total, :], dst_head.at[total, :], 1),
            remote(number, 1, src_rest.at[total, :], dst_rest.at[total, :], 1),
        )

    for which, ref in (
        ((row_id % HEAD).astype(F32), mix_head),
        ((HEAD + row_id % REST).astype(F32), mix_rest),
    ):
        value = jnp.where(slot == which, share, 0.0).T
        high = value.astype(BF)
        ref[0:toks, :] = high
        ref[toks:, :] = (value - high.astype(F32)).astype(BF)

    loads[-1].wait()
    swaps[0].wait()
    for n in range(wide // lanes):
        cols = slice(n * lanes, (n + 1) * lanes)

        def down_peak(i, best):
            at = pl.ds(pl.multiple_of(i * 16, 16), 16)
            return jnp.maximum(best, jnp.abs(down[at, cols].astype(F32)))

        best = lax.fori_loop(0, hidden_all // 16, down_peak, jnp.zeros((16, lanes), F32))
        peak = jnp.max(best, axis=0, keepdims=True) + 1e-06
        col_mul[:, cols] = jnp.broadcast_to(7.0 / peak, (8, lanes))
        col_div[:, cols] = jnp.broadcast_to(peak / 7.0, (8, lanes))

        def down_level(i, carry):
            at = pl.ds(pl.multiple_of(i * 16, 16), 16)
            value = down[at, cols].astype(F32)
            mul = jnp.concatenate((col_mul[:, cols], col_mul[:, cols]), axis=0)
            down_q[at, cols] = soft_level(value * mul).astype(BF)
            return carry

        lax.fori_loop(0, hidden_all // 16, down_level, 0)

    for s in range(ring):
        loads[2 * s].wait()
        loads[2 * s + 1].wait()
        swaps[1 + 2 * s].wait()
        swaps[2 + 2 * s].wait()
        for n in range(wide // lanes):
            cols = slice(n * lanes, (n + 1) * lanes)

            def weight_top(i, best):
                at = pl.ds(pl.multiple_of(i * 16, 16), 16)
                return jnp.maximum(best, jnp.abs(weight[s, at, cols].astype(F32)))

            best = lax.fori_loop(0, 2 * hid2 // 16, weight_top, jnp.zeros((16, lanes), F32))
            peak_own[s, :, cols] = jnp.broadcast_to(jnp.max(best, axis=0, keepdims=True), (8, lanes))

    def small(number, k, src, dst):
        return pltpu.make_async_remote_copy(
            src_ref=src,
            dst_ref=dst,
            send_sem=small_send.at[number, k - 1],
            recv_sem=small_recv.at[number, k - 1],
            device_id=along(k),
            device_id_type=MESH,
        )

    peak_copies = [
        small(0, k, peak_own.at[lax.rem(x + k, ring)], peak_in.at[k - 1]) for k in range(1, ring)
    ]
    for copy in peak_copies:
        copy.start()

    def far_copy(slot, src, dst, k):
        return pltpu.make_async_remote_copy(
            src_ref=src,
            dst_ref=dst,
            send_sem=far_send.at[slot],
            recv_sem=far_recv.at[slot],
            device_id=peer(k),
            device_id_type=MESH,
        )

    right_cols = slice(middle, wide)
    far_own = pl.ds(pl.multiple_of((me // 2) * HEAD, HEAD), HEAD)

    def far_owner(slot):
        return lax.rem(x + ring - 1 - slot, ring)

    @pl.when(odd)
    def _():
        for slot in range(ring - 1):
            far_tokens(slot + 1).wait()
            far_head[slot] = dot_nn(pick_head, tok_far[slot]).astype(BF)
            extra = jnp.zeros((n_head, eighth), F32)
            for q in range(4):
                extra = extra + dot_nn(
                    jnp.where(part_id == q, pick_rest, 0.0).astype(BF),
                    tok_far[slot, :, q * eighth : (q + 1) * eighth],
                )
            far_rest[:, slot * eighth : (slot + 1) * eighth] = extra.astype(BF)

        def far_dispatch(k, carry):
            to = at_group(lax.rem(me + k, groups))
            for slot in range(ring - 1):
                far_copy(
                    slot, far_head.at[slot, to, :], rows.at[far_owner(slot), landing_group(me), right_cols], k
                ).start()
            far_copy(ring - 1, far_rest.at[to, :], far_in.at[far_own, :], k).start()
            return carry

        lax.fori_loop(1, groups, far_dispatch, 0)
        for slot in range(ring - 1):
            rows[far_owner(slot), landing_group(me), right_cols] = far_head[slot, at_group(me), :]
        far_in[far_own, :] = far_rest[at_group(me), :]

    def far_arrive():
        for parity in range(min(2, gh)):

            @pl.when(side_of(me) == parity)
            def _():
                some = pl.ds(0, (gh - parity) * HEAD)
                for slot in range(ring - 1):
                    far_copy(slot, far_head.at[slot, some, :], rows.at[0, some, right_cols], 1).wait_recv()
                far_copy(ring - 1, far_rest.at[some, :], far_in.at[some, :], 1).wait_recv()

        near = iota((gh * REST, half_head), 1)
        base_row = iota((gh * REST, half_head), 0)
        same_row = (near // HEAD == base_row // REST) & (near % REST == base_row % REST)
        for q in range(4):
            order = (same_row & ((near // REST) % 4 == q)).astype(F32).astype(BF)
            moved = dot_nn(order, far_in[...]).astype(BF)
            for slot in range(ring - 1):
                rows[
                    far_owner(slot), half + half_head : 2 * half, middle + q * eighth : middle + (q + 1) * eighth
                ] = moved[:, slot * eighth : (slot + 1) * eighth]

    for copy in peak_copies:
        copy.wait()
    weight_peak = peak_own[x]
    for k in range(1, ring):
        weight_peak = jnp.maximum(weight_peak, peak_in[k - 1])

    def ring_copy(number, ref, h, way, step, mag, to):
        if way == 0:
            owner = lax.rem(x - mag + ring, ring)
            part_of = step % 2
        else:
            owner = lax.rem(x + mag, ring)
            part_of = 1 - step % 2
        at = pl.ds(h * half + part_of * piece_rows, piece_rows)
        if ref is rows:
            piece = ref.at[owner, at, pl.ds((number // 3) * middle, middle)]
        else:
            piece = ref.at[owner, at, :]
        return pltpu.make_async_remote_copy(
            src_ref=piece,
            dst_ref=piece,
            send_sem=ring_send.at[number, h, way, step],
            recv_sem=ring_recv.at[number, h, way, step],
            device_id=along(to),
            device_id_type=MESH,
        )

    def hop(number, ref, h, way, step):
        return ring_copy(number, ref, h, way, step, step // 2, 1 if way == 0 else ring - 1)

    def landed(number, ref, h, way, step):
        return ring_copy(number, ref, h, way, step, 1 + step // 2, 1)

    def launch(number, ref, h, steps):
        for step in steps:
            for way in range(2):
                hop(number, ref, h, way, step).start()

    def await_step(number, ref, h, step):
        for way in range(2):
            landed(number, ref, h, way, step).wait_recv()

    def relay(number, ref, h):
        for way in range(2):
            landed(number, ref, h, way, 0).wait_recv()
            hop(number, ref, h, way, 2).start()

    def drain(number, ref):
        for h in range(1 if number == 3 else 2):
            for step in range(3):
                for way in range(2):
                    hop(number, ref, h, way, step).wait_send()

    pltpu.make_async_remote_copy(
        src_ref=top_send.at[pl.ds(0, (groups - 1) * tiles), :],
        dst_ref=top_in.at[pl.ds(0, (groups - 1) * tiles), :],
        send_sem=a2a_send.at[4, 0],
        recv_sem=a2a_recv.at[4, 0],
        device_id=peer(1),
        device_id_type=MESH,
    ).wait()
    act_peak = top_in[0:tiles, :]
    for g in range(1, groups):
        act_peak = jnp.maximum(act_peak, top_in[g * tiles : (g + 1) * tiles, :])
    act_peak = jnp.maximum(act_peak, 1.0)
    for n in range(tiles):
        cols = slice(n * 128, (n + 1) * 128)
        smooth[x, :, cols] = jnp.sqrt(act_peak[n : n + 1, :] / (weight_peak[:, cols] + 1e-06))
    smooth_copies = [small(1, k, smooth.at[x], smooth.at[x]) for k in range(1, ring)]
    for copy in smooth_copies:
        copy.start()
    for copy in smooth_copies:
        copy.wait()
    for s in range(ring):
        inv_smooth[s, :, :] = 1.0 / smooth[s]

    spread = iota((gh * REST, n_head), 1)
    home = iota((gh * REST, n_head), 0)

    def arrive(side):
        for copy in sent[side]:
            copy.wait_send()
            copy.wait_recv()
        for h in range(2):
            same_row = (spread // HEAD == 2 * (home // REST) + (h + home // (4 * REST)) % 2) & (spread % REST == home % REST)
            for q in range(4):
                order = (same_row & ((spread // REST) % 4 == q)).astype(F32).astype(BF)
                slab[
                    h * half + half_head : (h + 1) * half,
                    side * middle + q * eighth : side * middle + (q + 1) * eighth,
                ] = dot_nn(order, rest_in[:, side * eighth : (side + 1) * eighth]).astype(BF)

    arrive(0)
    launch(0, rows, 0, (0, 1))

    def weight_level(i, carry):
        at = pl.ds(pl.multiple_of(i * 16, 16), 16)
        best = jnp.zeros((16, lanes), F32)
        for s in range(ring):
            for n in range(wide // lanes):
                cols = slice(n * lanes, (n + 1) * lanes)
                best = jnp.maximum(best, jnp.abs(weight[s, at, cols].astype(F32) * smooth[s, 0:1, cols]))
        peak = jnp.max(best, axis=1, keepdims=True) + 1e-06
        mul = 7.0 / peak
        div = peak / 7.0
        for s in range(ring):
            for n in range(wide // lanes):
                cols = slice(n * lanes, (n + 1) * lanes)
                value = weight[s, at, cols].astype(F32) * smooth[s, 0:1, cols]
                weight_q[s, at, cols] = (div * soft_level(value * mul)).astype(BF)
        return carry

    n_strip = 2 * hid2 // 16
    lax.fori_loop(0, n_strip // 2, weight_level, 0)
    relay(0, rows, 0)
    launch(0, rows, 1, (0,))
    lax.fori_loop(n_strip // 2, n_strip, weight_level, 0)

    arrive(1)
    eye = iota((block, block), 0) == iota((block, block), 1)
    top_rows = []
    for b in range(n_block):
        best = jnp.zeros((block, 128), F32)
        for n in range(tiles):
            cols = slice(n * 128, (n + 1) * 128)
            value = rows[x, b * block : (b + 1) * block, cols].astype(F32) * inv_smooth[x, 0:1, cols]
            best = jnp.maximum(best, jnp.abs(value))
        tall = jnp.max(best, axis=1, keepdims=True)
        top_rows.append(jnp.sum(jnp.where(eye, tall, 0.0), axis=0, keepdims=True))
    row_peak[x] = jnp.zeros((8, block), F32)
    for b in range(n_block):
        row_peak[x, b : b + 1, :] = top_rows[b]
    peak_rows = [small(2, k, row_peak.at[x], row_peak.at[x]) for k in range(1, ring)]
    for copy in peak_rows:
        copy.start()
    launch(3, rows, 0, (0, 1))

    strip = 16 if half % 16 == 0 else half

    def use_float(owner, h, first):
        at = pl.ds(h * half, half)
        product = dot_nt(rows[owner, at, :], weight[owner])
        acc_float[at, :] = product if first else acc_float[at, :] + product

    def level_rows(owner, h, out):
        for i in range(half // strip):
            here = slice(h * half + i * strip, h * half + (i + 1) * strip)
            mul = row_mul[here, 0:1]
            div = row_div[here, 0:1]
            for n in range(wide // lanes):
                cols = slice(n * lanes, (n + 1) * lanes)
                value = rows[owner, here, cols].astype(F32) * inv_smooth[owner, 0:1, cols]
                out[i * strip : (i + 1) * strip, cols] = (div * soft_level(value * mul)).astype(BF)

    def use_quant(owner, h, first, buf):
        at = pl.ds(h * half, half)
        product = dot_nt(buf[...], weight_q[owner])
        acc_quant[at, :] = product if first else acc_quant[at, :] + product

    def use_pair(h):
        left = lax.rem(x + ring - 1, ring)
        right = lax.rem(x + 1, ring)
        await_step(0, rows, h, 1)
        if h == 0:
            await_step(3, rows, h, 1)
        use_float(left, h, False)
        level_rows(left, h, rows_q)
        use_float(right, h, False)
        level_rows(right, h, rows_q2)
        use_quant(left, h, False, rows_q)
        use_quant(right, h, False, rows_q2)

    def use_across(h):
        across = lax.rem(x + 2, ring)
        await_step(0, rows, h, 2)
        if h == 0:
            await_step(3, rows, h, 2)
        use_float(across, h, False)
        level_rows(across, h, rows_q)
        use_quant(across, h, False, rows_q)

    def activate(acc, out, h):
        def piece(i, carry):
            at = pl.ds(pl.multiple_of(h * half + i * strip, strip), strip)
            gate = acc[at, 0:hid2]
            up = acc[at, hid2:]
            out[x, at, :] = (gate / (1.0 + jnp.exp(-gate)) * up).astype(BF)
            return carry

        lax.fori_loop(0, half // strip, piece, 0)

    turn = iota((half_head, gh * REST), 0)
    base = iota((half_head, gh * REST), 1)
    back_row = (turn // HEAD == base // REST) & (turn % REST == base % REST)
    turn_part = (turn // REST) % 4

    def project(hidden, matrix, head, rest, h, scaled):
        rest_acc[...] = jnp.zeros_like(rest_acc)
        at = pl.ds(h * half, half)

        def piece(q, carry):
            cols = pl.ds(pl.multiple_of(q * quarter, quarter), quarter)
            total = dot_nn(hidden[0, at, :], matrix[0:hid2, cols])
            for s in range(1, ring):
                total = total + dot_nn(hidden[s, at, :], matrix[s * hid2 : (s + 1) * hid2, cols])
            if scaled:
                total = total * level_div[at, 0:1] * col_div[0:1, cols]
            total = total.astype(BF)
            head[h * half_head : (h + 1) * half_head, cols] = total[:half_head]
            order = (back_row & (turn_part == q)).astype(F32).astype(BF)
            rest_acc[...] += dot_nn(order, total[half_head:])
            return carry

        lax.fori_loop(0, 4, piece, 0)
        rest[h * half_head : (h + 1) * half_head, :] = rest_acc[...].astype(BF)

    def levels(h):
        def piece(i, carry):
            at = pl.ds(pl.multiple_of(h * half + i * strip, strip), strip)
            best = jnp.zeros((strip, hid2), F32)
            for s in range(ring):
                best = jnp.maximum(best, jnp.abs(hid_quant[s, at, :].astype(F32)))
            peak = jnp.max(best, axis=1, keepdims=True) + 1e-06
            mul = 7.0 / peak
            level_div[at, :] = jnp.broadcast_to(peak / 7.0, (strip, 128))
            for s in range(ring):
                hid_level[s, at, :] = soft_level(hid_quant[s, at, :].astype(F32) * mul).astype(BF)
            return carry

        lax.fori_loop(0, half // strip, piece, 0)

    use_float(x, 0, True)
    use_float(x, 1, True)
    for copy in peak_rows:
        copy.wait()
    best_row = row_peak[0]
    for s in range(1, ring):
        best_row = jnp.maximum(best_row, row_peak[s])
    for b in range(n_block):
        flat = jnp.broadcast_to(best_row[b : b + 1, :], (block, block))
        tall = jnp.sum(jnp.where(eye, flat, 0.0), axis=1, keepdims=True) + 1e-06
        row_mul[b * block : (b + 1) * block, :] = jnp.broadcast_to(7.0 / tall, (block, 128))
        row_div[b * block : (b + 1) * block, :] = jnp.broadcast_to(tall / 7.0, (block, 128))
    level_rows(x, 0, rows_q)
    use_quant(x, 0, True, rows_q)
    relay(3, rows, 0)
    launch(0, rows, 1, (1,))
    use_pair(0)
    use_across(0)
    activate(acc_float, hid_float, 0)
    launch(1, hid_float, 0, (0, 1))
    activate(acc_quant, hid_quant, 0)
    level_rows(x, 1, rows_q)
    use_quant(x, 1, True, rows_q)
    relay(1, hid_float, 0)
    launch(2, hid_quant, 0, (0, 1))
    relay(0, rows, 1)
    await_step(1, hid_float, 0, 1)
    await_step(1, hid_float, 0, 2)
    project(hid_float, down, outf_head, outf_rest, 0, False)
    send_back(1, 0, outf_head, outf_rest, backf_head, backf_rest)
    relay(2, hid_quant, 0)
    far_arrive()
    use_pair(1)
    await_step(2, hid_quant, 0, 1)
    await_step(2, hid_quant, 0, 2)
    levels(0)
    project(hid_level, down_q, outq_head, outq_rest, 0, True)
    send_back(2, 0, outq_head, outq_rest, backq_head, backq_rest)
    use_across(1)
    activate(acc_float, hid_float, 1)
    launch(1, hid_float, 1, (0, 1))
    activate(acc_quant, hid_quant, 1)
    relay(1, hid_float, 1)
    launch(2, hid_quant, 1, (0, 1))
    await_step(1, hid_float, 1, 1)
    await_step(1, hid_float, 1, 2)
    project(hid_float, down, outf_head, outf_rest, 1, False)
    send_back(1, 1, outf_head, outf_rest, backf_head, backf_rest)
    relay(2, hid_quant, 1)
    await_step(2, hid_quant, 1, 1)
    await_step(2, hid_quant, 1, 2)
    levels(1)
    project(hid_level, down_q, outq_head, outq_rest, 1, True)
    send_back(2, 1, outq_head, outq_rest, backq_head, backq_rest)
    sent_float = back(1, outf_head, outf_rest, backf_head, backf_rest)
    sent_quant = back(2, outq_head, outq_rest, backq_head, backq_rest)

    def combine(number, head, rest):
        mixed = dot_nn(mix_head[...], head[...])
        mixed = mixed[:toks] + mixed[toks:]
        quarter_of = (iota((2 * toks, n_head), 1) // REST) % 4
        for q in range(4):
            weights = jnp.where(quarter_of == q, mix_rest[...].astype(F32), 0.0).astype(BF)
            extra = dot_nn(weights, rest[...])
            cols = slice(q * quarter, (q + 1) * quarter)
            first = (q * quarter) // width
            inner = q * quarter - first * width
            part[number, first, :, inner : inner + quarter] = mixed[:, cols] + extra[:toks] + extra[toks:]
        copy = pltpu.make_async_remote_copy(
            src_ref=part.at[number, 1 - core],
            dst_ref=part_in.at[number],
            send_sem=ex_send.at[number],
            recv_sem=ex_recv.at[number],
            device_id=partner,
            device_id_type=MESH,
        )
        copy.start()
        return copy

    for copy in sent_float:
        copy.wait_recv()
    half_float = combine(0, backf_head, backf_rest)
    half_float.wait()
    both_ref[0] = part[0, core] + part_in[0]
    for copy in sent_quant:
        copy.wait_recv()
    half_quant = combine(1, backq_head, backq_rest)

    for copy in sent_float:
        copy.wait_send()
    for copy in sent_quant:
        copy.wait_send()

    @pl.when(odd)
    def _():
        for slot in range(ring - 1):
            far_copy(slot, far_head.at[slot, total, :], far_head.at[slot, total, :], 1).wait_send()
        far_copy(ring - 1, far_rest.at[total, :], far_rest.at[total, :], 1).wait_send()

    for number, ref in enumerate((rows, hid_float, hid_quant, rows)):
        drain(number, ref)
    half_quant.wait()
    both_ref[1] = part[1, core] + part_in[1]


def solution(mesh):
    groups = mesh.shape["dp"]
    ring = mesh.shape["expert"] // 2

    def on_device(tokens, expert_ids, route_weights, gate_weight, up_weight, down_weight):
        toks, width = tokens.shape
        wide = 2 * width
        quarter = wide // 4
        hid = gate_weight.shape[1]
        hid2 = 2 * hid
        count = groups * CAP
        half = count // 2
        n_head = groups * HEAD
        hidden_all = ring * hid2
        block = 128 if count % 128 == 0 else count
        vmem = pltpu.VMEM
        dma = pltpu.SemaphoreType.DMA
        here = pl.BlockSpec(memory_space=pltpu.VMEM)
        away = pl.BlockSpec(memory_space=pl.ANY)
        both = pl.pallas_call(
            functools.partial(layer_kernel, groups, ring),
            name="moe_layer",
            out_shape=jax.ShapeDtypeStruct((2, toks, width), F32),
            in_specs=[here, here, here, away, away, away],
            out_specs=here,
            scratch_shapes=[
                vmem((toks, wide), BF),
                vmem((n_head, wide), BF),
                vmem((n_head, quarter), BF),
                vmem((ring, count, wide), BF),
                vmem((n_head, quarter), BF),
                vmem((ring, 2 * hid2, wide), BF),
                vmem((ring, 2 * hid2, wide), BF),
                vmem((hidden_all, wide), BF),
                vmem((hidden_all, wide), BF),
                vmem((half, wide), BF),
                vmem((half, wide), BF),
                vmem((count, 2 * hid2), F32),
                vmem((count, 2 * hid2), F32),
                vmem((ring, count, hid2), BF),
                vmem((ring, count, hid2), BF),
                vmem((ring, count, hid2), BF),
                vmem((ring, 8, wide), F32),
                vmem((ring - 1, 8, wide), F32),
                vmem((ring, 8, wide), F32),
                vmem((ring, 8, wide), F32),
                vmem((ring, 8, block), F32),
                vmem((count, 128), F32),
                vmem((count, 128), F32),
                vmem((count, 128), F32),
                vmem((8, wide), F32),
                vmem((8, wide), F32),
                vmem((groups * (wide // 128), 128), F32),
                vmem((groups * (wide // 128), 128), F32),
                vmem((2 * toks, n_head), BF),
                vmem((2 * toks, n_head), BF),
                vmem((n_head, wide), BF),
                vmem((n_head, quarter), BF),
                vmem((n_head, wide), BF),
                vmem((n_head, quarter), BF),
                vmem((n_head // 2, quarter), F32),
                vmem((n_head, wide), BF),
                vmem((n_head, quarter), BF),
                vmem((n_head, wide), BF),
                vmem((n_head, quarter), BF),
                vmem((2, 2, toks, width), F32),
                vmem((2, toks, width), F32),
                vmem((ring - 1, toks, wide // 2), BF),
                vmem((ring - 1, n_head, wide // 2), BF),
                vmem((n_head, (ring - 1) * quarter // 2), BF),
                vmem((n_head // 2, (ring - 1) * quarter // 2), BF),
                dma((ring - 1,)),
                dma((ring - 1,)),
                dma((ring,)),
                dma((ring,)),
                dma((2 * ring + 1,)),
                dma((2 + 2 * ring,)),
                dma((2 + 2 * ring,)),
                dma((5, 2)),
                dma((5, 2)),
                dma((3, ring - 1)),
                dma((3, ring - 1)),
                dma((4, 2, 2, 3)),
                dma((4, 2, 2, 3)),
                dma((2,)),
                dma((2,)),
            ],
            compiler_params=pltpu.CompilerParams(
                collective_id=0, has_side_effects=True, vmem_limit_bytes=64 * 1024 * 1024 - 128 * 1024
            ),
        )(
            tokens,
            expert_ids.T,
            route_weights.T,
            gate_weight,
            up_weight,
            down_weight,
        )
        return both[1].astype(BF), both[0]

    in_specs = (
        P("dp", "expert"),
        P("dp", None),
        P("dp", None),
        P("dp", "expert", None),
        P("dp", "expert", None),
        P("dp", None, "expert"),
    )
    out_specs = (P("dp", "expert"), P("dp", "expert"))
    return jax.shard_map(
        on_device, mesh=mesh, in_specs=in_specs, out_specs=out_specs, check_vma=False
    )
```

```python
import functools

import jax
import jax.numpy as jnp
from jax import lax
from jax.experimental import pallas as pl
from jax.experimental.pallas import tpu as pltpu
from jax.sharding import PartitionSpec as P

MESH = pl.DeviceIdType.MESH
CAP = 20
HEAD = 16
REST = CAP - HEAD
BF = jnp.bfloat16
F32 = jnp.float32
COEF = (6.5788915972740805, -12.960054087409885, 11.90224462767755, -5.297839452865238)
ROUND = 12582912.0


def soft_level(values):
    whole = (values + ROUND) - ROUND
    rest = values - whole
    square = rest * rest
    poly = COEF[-1]
    for coef in COEF[-2::-1]:
        poly = poly * square + coef
    return whole + (rest * square) * poly


def dot_nt(a, b):
    return lax.dot_general(a, b, (((1,), (1,)), ((), ())), preferred_element_type=F32)


def dot_nn(a, b):
    return lax.dot_general(a, b, (((1,), (0,)), ((), ())), preferred_element_type=F32)


def iota(shape, axis):
    return lax.broadcasted_iota(jnp.int32, shape, axis)


def layer_kernel(
    groups,
    ring,
    tok_ref,
    ids_t_ref,
    route_ref,
    gate_hbm,
    up_hbm,
    down_hbm,
    both_ref,
    tok,
    send_head,
    send_rest,
    rows,
    rest_in,
    weight,
    weight_q,
    down,
    down_q,
    rows_q,
    rows_q2,
    acc_float,
    acc_quant,
    hid_float,
    hid_quant,
    hid_level,
    peak_own,
    peak_in,
    smooth,
    inv_smooth,
    row_peak,
    row_mul,
    row_div,
    level_div,
    col_mul,
    col_div,
    top_send,
    top_in,
    mix_head,
    mix_rest,
    outf_head,
    outf_rest,
    outq_head,
    outq_rest,
    rest_acc,
    backf_head,
    backf_rest,
    backq_head,
    backq_rest,
    part,
    part_in,
    tok_far,
    far_head,
    far_rest,
    far_in,
    tok_send,
    tok_recv,
    far_send,
    far_recv,
    load_sem,
    swap_send,
    swap_recv,
    a2a_send,
    a2a_recv,
    small_send,
    small_recv,
    ring_send,
    ring_recv,
    ex_send,
    ex_recv,
):
    me = lax.axis_index("dp")
    seat = lax.axis_index("expert")
    x = seat // 2
    core = seat % 2
    width = tok_ref.shape[1]
    wide = 2 * width
    quarter = wide // 4
    hid = gate_hbm.shape[1]
    hid2 = 2 * hid
    count = groups * CAP
    half = count // 2
    n_head = groups * HEAD
    gh = groups // 2
    half_head = gh * HEAD
    piece_rows = half // 2
    top = ids_t_ref.shape[0]
    toks = tok_ref.shape[0]
    lanes = min(512, wide)
    block = 128 if count % 128 == 0 else count
    n_block = count // block
    hidden_all = ring * hid2

    partner = (me, x * 2 + 1 - core)

    def along(k):
        return (me, lax.rem(x + k, ring) * 2 + core)

    def peer(k):
        return (lax.rem(me + k, groups), seat)

    loads = []
    for s in range(ring):
        for g, src in enumerate((gate_hbm, up_hbm)):
            loads.append(
                pltpu.make_async_copy(
                    src.at[core, :, pl.ds(s * wide, wide)],
                    weight.at[s, pl.ds(pl.multiple_of(g * hid2 + core * hid, 8), hid), :],
                    load_sem.at[2 * s + g],
                )
            )
    loads.append(
        pltpu.make_async_copy(
            down_hbm.at[core],
            down.at[:, pl.ds(pl.multiple_of(core * width, 128), width)],
            load_sem.at[2 * ring],
        )
    )
    loads[-1].start()
    for copy in loads[:-1]:
        copy.start()

    barrier = pltpu.get_barrier_semaphore()
    pl.semaphore_signal(barrier, inc=1, device_id=partner, device_id_type=MESH)
    for k in range(1, ring):
        pl.semaphore_signal(barrier, inc=1, device_id=along(k), device_id_type=MESH)

    def greet(k, carry):
        pl.semaphore_signal(barrier, inc=1, device_id=peer(k), device_id_type=MESH)
        return carry

    lax.fori_loop(1, groups, greet, 0)

    before = (iota((toks, toks), 0) < iota((toks, toks), 1)).astype(BF)
    row_id = iota((n_head, toks), 0)
    hit = jnp.zeros((n_head, toks), F32)
    wanted = (row_id // HEAD) * 2 + core
    share = jnp.zeros((n_head, toks), F32)
    ratio = route_ref[...]
    ratio = ratio / jnp.sum(ratio, axis=0, keepdims=True)
    for k in range(top):
        same = ids_t_ref[k : k + 1, :] == wanted
        hit = hit + same.astype(F32)
        share = share + jnp.where(same, ratio[k : k + 1, :], 0.0)
    slot = dot_nn(hit.astype(BF), before)
    pick_head = jnp.where(slot == (row_id % HEAD).astype(F32), hit, 0.0).astype(BF)
    pick_rest = jnp.where(slot == (HEAD + row_id % REST).astype(F32), hit, 0.0)
    part_id = (row_id // REST) % 4
    hit_group = jnp.zeros((groups, toks), F32)
    wanted = iota((groups, toks), 0) * 2 + core
    for k in range(top):
        hit_group = hit_group + (ids_t_ref[k : k + 1, :] == wanted).astype(F32)
    slot_group = dot_nn(hit_group.astype(BF), before)
    pick_all = jnp.concatenate(
        [jnp.where(slot_group == float(n), hit_group, 0.0).astype(BF) for n in range(CAP)], axis=0
    )
    tiles = wide // 128
    eighth = quarter // 2
    middle = wide // 2

    pl.semaphore_wait(barrier, 1 + (ring - 1) + (groups - 1))

    own_cols = pl.ds(pl.multiple_of(core * width, 128), width)
    tok_copy = pltpu.make_async_remote_copy(
        src_ref=tok_ref,
        dst_ref=tok.at[:, own_cols],
        send_sem=swap_send.at[0],
        recv_sem=swap_recv.at[0],
        device_id=partner,
        device_id_type=MESH,
    )
    tok_copy.start()
    tok[:, own_cols] = tok_ref[...]
    swaps = [
        pltpu.make_async_remote_copy(
            src_ref=down_hbm.at[1 - core],
            dst_ref=down.at[:, own_cols],
            send_sem=swap_send.at[1],
            recv_sem=swap_recv.at[1],
            device_id=partner,
            device_id_type=MESH,
        )
    ]
    for s in range(ring):
        for g, src in enumerate((gate_hbm, up_hbm)):
            swaps.append(
                pltpu.make_async_remote_copy(
                    src_ref=src.at[1 - core, :, pl.ds(s * wide, wide)],
                    dst_ref=weight.at[s, pl.ds(pl.multiple_of(g * hid2 + core * hid, 8), hid), :],
                    send_sem=swap_send.at[2 + 2 * s + g],
                    recv_sem=swap_recv.at[2 + 2 * s + g],
                    device_id=partner,
                    device_id_type=MESH,
                )
            )
    tok_copy.wait()
    odd = (me + me // 8) % 2 == 1

    def far_tokens(k):
        return pltpu.make_async_remote_copy(
            src_ref=tok.at[:, pl.ds(wide // 2, wide // 2)],
            dst_ref=tok_far.at[k - 1],
            send_sem=tok_send.at[k - 1],
            recv_sem=tok_recv.at[k - 1],
            device_id=along(k),
            device_id_type=MESH,
        )

    @pl.when(odd)
    def _():
        for k in range(1, ring):
            far_tokens(k).start()

    for copy in swaps:
        copy.start()

    every = jnp.abs(dot_nn(pick_all, tok[...]))
    highest = every[0:groups]
    for n in range(1, CAP):
        highest = jnp.maximum(highest, every[n * groups : (n + 1) * groups])
    for n in range(tiles):
        top_send[pl.ds(n, groups, stride=tiles), :] = highest[:, n * 128 : (n + 1) * 128]

    def top_at(g):
        return pl.ds(pl.multiple_of(g * tiles, tiles), tiles)

    def send_top(k, carry):
        pltpu.make_async_remote_copy(
            src_ref=top_send.at[top_at(lax.rem(me + k, groups)), :],
            dst_ref=top_in.at[top_at(me), :],
            send_sem=a2a_send.at[4, 0],
            recv_sem=a2a_recv.at[4, 0],
            device_id=peer(k),
            device_id_type=MESH,
        ).start()
        return carry

    lax.fori_loop(1, groups, send_top, 0)
    top_in[top_at(me), :] = top_send[top_at(me), :]

    send_head[...] = dot_nn(pick_head, tok[...]).astype(BF)
    chosen = jnp.zeros((n_head, quarter), F32)
    for q in range(4):
        pair = jnp.concatenate(
            (
                tok[:, q * eighth : (q + 1) * eighth],
                tok[:, middle + q * eighth : middle + (q + 1) * eighth],
            ),
            axis=1,
        )
        chosen = chosen + dot_nn(jnp.where(part_id == q, pick_rest, 0.0).astype(BF), pair)
    send_rest[...] = chosen.astype(BF)

    def side_of(g):
        return (g + g // 8) % 2

    def at_group(g):
        return pl.ds(pl.multiple_of(g * HEAD, HEAD), HEAD)

    def split_group(g):
        return pl.ds(pl.multiple_of(side_of(g) * half_head + (g // 2) * HEAD, HEAD), HEAD)

    def landing_group(g):
        return pl.ds(pl.multiple_of(side_of(g) * half + (g // 2) * HEAD, HEAD), HEAD)

    def remote(number, index, src, dst, k):
        return pltpu.make_async_remote_copy(
            src_ref=src,
            dst_ref=dst,
            send_sem=a2a_send.at[number, index],
            recv_sem=a2a_recv.at[number, index],
            device_id=peer(k),
            device_id_type=MESH,
        )

    total = pl.ds(0, (groups - 1) * HEAD)

    slab = rows.at[x]

    sent = []
    for side in range(2):
        cols = slice(side * middle, (side + 1) * middle)
        thin = slice(side * eighth, (side + 1) * eighth)
        number = 3 * side

        def dispatch(k, carry):
            to = at_group(lax.rem(me + k, groups))
            remote(number, 0, send_head.at[to, cols], slab.at[landing_group(me), cols], k).start()
            remote(number, 1, send_rest.at[to, thin], rest_in.at[at_group(me), thin], k).start()
            return carry

        lax.fori_loop(1, groups, dispatch, 0)
        sent.append(
            (
                remote(number, 0, send_head.at[total, cols], slab.at[total, cols], 1),
                remote(number, 1, send_rest.at[total, thin], rest_in.at[total, thin], 1),
            )
        )
    slab[landing_group(me), :] = send_head[at_group(me), :]
    rest_in[at_group(me), :] = send_rest[at_group(me), :]

    def send_back(number, part_of, src_head, src_rest, dst_head, dst_rest):
        def begin(i, carry):
            pair = lax.rem(me // 2 + i, gh)
            to = 2 * pair + (part_of + pair // 4) % 2

            @pl.when(to != me)
            def _():
                at = split_group(to)
                k = to - me + groups
                remote(number, 0, src_head.at[at, :], dst_head.at[at_group(me), :], k).start()
                remote(number, 1, src_rest.at[at, :], dst_rest.at[at_group(me), :], k).start()

            return carry

        lax.fori_loop(1, gh + 1, begin, 0)

        @pl.when(side_of(me) == part_of)
        def _():
            dst_head[at_group(me), :] = src_head[split_group(me), :]
            dst_rest[at_group(me), :] = src_rest[split_group(me), :]

    def back(number, src_head, src_rest, dst_head, dst_rest):
        return (
            remote(number, 0, src_head.at[total, :], dst_head.at[total, :], 1),
            remote(number, 1, src_rest.at[total, :], dst_rest.at[total, :], 1),
        )

    for which, ref in (
        ((row_id % HEAD).astype(F32), mix_head),
        ((HEAD + row_id % REST).astype(F32), mix_rest),
    ):
        value = jnp.where(slot == which, share, 0.0).T
        high = value.astype(BF)
        ref[0:toks, :] = high
        ref[toks:, :] = (value - high.astype(F32)).astype(BF)

    loads[-1].wait()
    swaps[0].wait()
    for n in range(wide // lanes):
        cols = slice(n * lanes, (n + 1) * lanes)

        def down_peak(i, best):
            at = pl.ds(pl.multiple_of(i * 16, 16), 16)
            return jnp.maximum(best, jnp.abs(down[at, cols].astype(F32)))

        best = lax.fori_loop(0, hidden_all // 16, down_peak, jnp.zeros((16, lanes), F32))
        peak = jnp.max(best, axis=0, keepdims=True) + 1e-06
        col_mul[:, cols] = jnp.broadcast_to(7.0 / peak, (8, lanes))
        col_div[:, cols] = jnp.broadcast_to(peak / 7.0, (8, lanes))

        def down_level(i, carry):
            at = pl.ds(pl.multiple_of(i * 16, 16), 16)
            value = down[at, cols].astype(F32)
            mul = jnp.concatenate((col_mul[:, cols], col_mul[:, cols]), axis=0)
            down_q[at, cols] = soft_level(value * mul).astype(BF)
            return carry

        lax.fori_loop(0, hidden_all // 16, down_level, 0)

    for s in range(ring):
        loads[2 * s].wait()
        loads[2 * s + 1].wait()
        swaps[1 + 2 * s].wait()
        swaps[2 + 2 * s].wait()
        for n in range(wide // lanes):
            cols = slice(n * lanes, (n + 1) * lanes)

            def weight_top(i, best):
                at = pl.ds(pl.multiple_of(i * 16, 16), 16)
                return jnp.maximum(best, jnp.abs(weight[s, at, cols].astype(F32)))

            best = lax.fori_loop(0, 2 * hid2 // 16, weight_top, jnp.zeros((16, lanes), F32))
            peak_own[s, :, cols] = jnp.broadcast_to(jnp.max(best, axis=0, keepdims=True), (8, lanes))

    def small(number, k, src, dst):
        return pltpu.make_async_remote_copy(
            src_ref=src,
            dst_ref=dst,
            send_sem=small_send.at[number, k - 1],
            recv_sem=small_recv.at[number, k - 1],
            device_id=along(k),
            device_id_type=MESH,
        )

    peak_copies = [
        small(0, k, peak_own.at[lax.rem(x + k, ring)], peak_in.at[k - 1]) for k in range(1, ring)
    ]
    for copy in peak_copies:
        copy.start()

    def far_copy(slot, src, dst, k):
        return pltpu.make_async_remote_copy(
            src_ref=src,
            dst_ref=dst,
            send_sem=far_send.at[slot],
            recv_sem=far_recv.at[slot],
            device_id=peer(k),
            device_id_type=MESH,
        )

    right_cols = slice(middle, wide)
    far_own = pl.ds(pl.multiple_of((me // 2) * HEAD, HEAD), HEAD)

    def far_owner(slot):
        return lax.rem(x + ring - 1 - slot, ring)

    @pl.when(odd)
    def _():
        for slot in range(ring - 1):
            far_tokens(slot + 1).wait()
            far_head[slot] = dot_nn(pick_head, tok_far[slot]).astype(BF)
            extra = jnp.zeros((n_head, eighth), F32)
            for q in range(4):
                extra = extra + dot_nn(
                    jnp.where(part_id == q, pick_rest, 0.0).astype(BF),
                    tok_far[slot, :, q * eighth : (q + 1) * eighth],
                )
            far_rest[:, slot * eighth : (slot + 1) * eighth] = extra.astype(BF)

        def far_dispatch(k, carry):
            to = at_group(lax.rem(me + k, groups))
            for slot in range(ring - 1):
                far_copy(
                    slot, far_head.at[slot, to, :], rows.at[far_owner(slot), landing_group(me), right_cols], k
                ).start()
            far_copy(ring - 1, far_rest.at[to, :], far_in.at[far_own, :], k).start()
            return carry

        lax.fori_loop(1, groups, far_dispatch, 0)
        for slot in range(ring - 1):
            rows[far_owner(slot), landing_group(me), right_cols] = far_head[slot, at_group(me), :]
        far_in[far_own, :] = far_rest[at_group(me), :]

    def far_arrive():
        for parity in range(min(2, gh)):

            @pl.when(side_of(me) == parity)
            def _():
                some = pl.ds(0, (gh - parity) * HEAD)
                for slot in range(ring - 1):
                    far_copy(slot, far_head.at[slot, some, :], rows.at[0, some, right_cols], 1).wait_recv()
                far_copy(ring - 1, far_rest.at[some, :], far_in.at[some, :], 1).wait_recv()

        near = iota((gh * REST, half_head), 1)
        base_row = iota((gh * REST, half_head), 0)
        same_row = (near // HEAD == base_row // REST) & (near % REST == base_row % REST)
        for q in range(4):
            order = (same_row & ((near // REST) % 4 == q)).astype(F32).astype(BF)
            moved = dot_nn(order, far_in[...]).astype(BF)
            for slot in range(ring - 1):
                rows[
                    far_owner(slot), half + half_head : 2 * half, middle + q * eighth : middle + (q + 1) * eighth
                ] = moved[:, slot * eighth : (slot + 1) * eighth]

    for copy in peak_copies:
        copy.wait()
    weight_peak = peak_own[x]
    for k in range(1, ring):
        weight_peak = jnp.maximum(weight_peak, peak_in[k - 1])

    def ring_copy(number, ref, h, way, step, mag, to):
        if way == 0:
            owner = lax.rem(x - mag + ring, ring)
            part_of = step % 2
        else:
            owner = lax.rem(x + mag, ring)
            part_of = 1 - step % 2
        at = pl.ds(h * half + part_of * piece_rows, piece_rows)
        if ref is rows:
            piece = ref.at[owner, at, pl.ds((number // 3) * middle, middle)]
        else:
            piece = ref.at[owner, at, :]
        return pltpu.make_async_remote_copy(
            src_ref=piece,
            dst_ref=piece,
            send_sem=ring_send.at[number, h, way, step],
            recv_sem=ring_recv.at[number, h, way, step],
            device_id=along(to),
            device_id_type=MESH,
        )

    def hop(number, ref, h, way, step):
        return ring_copy(number, ref, h, way, step, step // 2, 1 if way == 0 else ring - 1)

    def landed(number, ref, h, way, step):
        return ring_copy(number, ref, h, way, step, 1 + step // 2, 1)

    def launch(number, ref, h, steps):
        for step in steps:
            for way in range(2):
                hop(number, ref, h, way, step).start()

    def await_step(number, ref, h, step):
        for way in range(2):
            landed(number, ref, h, way, step).wait_recv()

    def relay(number, ref, h):
        for way in range(2):
            landed(number, ref, h, way, 0).wait_recv()
            hop(number, ref, h, way, 2).start()

    def drain(number, ref):
        for h in range(1 if number == 3 else 2):
            for step in range(3):
                for way in range(2):
                    hop(number, ref, h, way, step).wait_send()

    pltpu.make_async_remote_copy(
        src_ref=top_send.at[pl.ds(0, (groups - 1) * tiles), :],
        dst_ref=top_in.at[pl.ds(0, (groups - 1) * tiles), :],
        send_sem=a2a_send.at[4, 0],
        recv_sem=a2a_recv.at[4, 0],
        device_id=peer(1),
        device_id_type=MESH,
    ).wait()
    act_peak = top_in[0:tiles, :]
    for g in range(1, groups):
        act_peak = jnp.maximum(act_peak, top_in[g * tiles : (g + 1) * tiles, :])
    act_peak = jnp.maximum(act_peak, 1.0)
    for n in range(tiles):
        cols = slice(n * 128, (n + 1) * 128)
        smooth[x, :, cols] = jnp.sqrt(act_peak[n : n + 1, :] / (weight_peak[:, cols] + 1e-06))
    smooth_copies = [small(1, k, smooth.at[x], smooth.at[x]) for k in range(1, ring)]
    for copy in smooth_copies:
        copy.start()
    for copy in smooth_copies:
        copy.wait()
    for s in range(ring):
        inv_smooth[s, :, :] = 1.0 / smooth[s]

    spread = iota((gh * REST, n_head), 1)
    home = iota((gh * REST, n_head), 0)

    def arrive(side):
        for copy in sent[side]:
            copy.wait_send()
            copy.wait_recv()
        for h in range(2):
            same_row = (spread // HEAD == 2 * (home // REST) + (h + home // (4 * REST)) % 2) & (spread % REST == home % REST)
            for q in range(4):
                order = (same_row & ((spread // REST) % 4 == q)).astype(F32).astype(BF)
                slab[
                    h * half + half_head : (h + 1) * half,
                    side * middle + q * eighth : side * middle + (q + 1) * eighth,
                ] = dot_nn(order, rest_in[:, side * eighth : (side + 1) * eighth]).astype(BF)

    arrive(0)
    launch(0, rows, 0, (0, 1))

    def weight_level(i, carry):
        at = pl.ds(pl.multiple_of(i * 16, 16), 16)
        best = jnp.zeros((16, lanes), F32)
        for s in range(ring):
            for n in range(wide // lanes):
                cols = slice(n * lanes, (n + 1) * lanes)
                best = jnp.maximum(best, jnp.abs(weight[s, at, cols].astype(F32) * smooth[s, 0:1, cols]))
        peak = jnp.max(best, axis=1, keepdims=True) + 1e-06
        mul = 7.0 / peak
        div = peak / 7.0
        for s in range(ring):
            for n in range(wide // lanes):
                cols = slice(n * lanes, (n + 1) * lanes)
                value = weight[s, at, cols].astype(F32) * smooth[s, 0:1, cols]
                weight_q[s, at, cols] = (div * soft_level(value * mul)).astype(BF)
        return carry

    n_strip = 2 * hid2 // 16
    lax.fori_loop(0, n_strip // 2, weight_level, 0)
    relay(0, rows, 0)
    launch(0, rows, 1, (0,))
    lax.fori_loop(n_strip // 2, n_strip, weight_level, 0)

    arrive(1)
    eye = iota((block, block), 0) == iota((block, block), 1)
    top_rows = []
    for b in range(n_block):
        best = jnp.zeros((block, 128), F32)
        for n in range(tiles):
            cols = slice(n * 128, (n + 1) * 128)
            value = rows[x, b * block : (b + 1) * block, cols].astype(F32) * inv_smooth[x, 0:1, cols]
            best = jnp.maximum(best, jnp.abs(value))
        tall = jnp.max(best, axis=1, keepdims=True)
        top_rows.append(jnp.sum(jnp.where(eye, tall, 0.0), axis=0, keepdims=True))
    row_peak[x] = jnp.zeros((8, block), F32)
    for b in range(n_block):
        row_peak[x, b : b + 1, :] = top_rows[b]
    peak_rows = [small(2, k, row_peak.at[x], row_peak.at[x]) for k in range(1, ring)]
    for copy in peak_rows:
        copy.start()
    launch(3, rows, 0, (0, 1))

    strip = 16 if half % 16 == 0 else half

    def use_float(owner, h, first):
        at = pl.ds(h * half, half)
        product = dot_nt(rows[owner, at, :], weight[owner])
        acc_float[at, :] = product if first else acc_float[at, :] + product

    def level_rows(owner, h, out):
        for i in range(half // strip):
            here = slice(h * half + i * strip, h * half + (i + 1) * strip)
            mul = row_mul[here, 0:1]
            div = row_div[here, 0:1]
            for n in range(wide // lanes):
                cols = slice(n * lanes, (n + 1) * lanes)
                value = rows[owner, here, cols].astype(F32) * inv_smooth[owner, 0:1, cols]
                out[i * strip : (i + 1) * strip, cols] = (div * soft_level(value * mul)).astype(BF)

    def use_quant(owner, h, first, buf):
        at = pl.ds(h * half, half)
        product = dot_nt(buf[...], weight_q[owner])
        acc_quant[at, :] = product if first else acc_quant[at, :] + product

    def use_pair(h):
        left = lax.rem(x + ring - 1, ring)
        right = lax.rem(x + 1, ring)
        await_step(0, rows, h, 1)
        if h == 0:
            await_step(3, rows, h, 1)
        use_float(left, h, False)
        level_rows(left, h, rows_q)
        use_float(right, h, False)
        level_rows(right, h, rows_q2)
        use_quant(left, h, False, rows_q)
        use_quant(right, h, False, rows_q2)

    def use_across(h):
        across = lax.rem(x + 2, ring)
        await_step(0, rows, h, 2)
        if h == 0:
            await_step(3, rows, h, 2)
        use_float(across, h, False)
        level_rows(across, h, rows_q)
        use_quant(across, h, False, rows_q)

    def activate(acc, out, h):
        def piece(i, carry):
            at = pl.ds(pl.multiple_of(h * half + i * strip, strip), strip)
            gate = acc[at, 0:hid2]
            up = acc[at, hid2:]
            out[x, at, :] = (gate / (1.0 + jnp.exp(-gate)) * up).astype(BF)
            return carry

        lax.fori_loop(0, half // strip, piece, 0)

    turn = iota((half_head, gh * REST), 0)
    base = iota((half_head, gh * REST), 1)
    back_row = (turn // HEAD == base // REST) & (turn % REST == base % REST)
    turn_part = (turn // REST) % 4

    def project(hidden, matrix, head, rest, h, scaled):
        rest_acc[...] = jnp.zeros_like(rest_acc)
        at = pl.ds(h * half, half)

        def piece(q, carry):
            cols = pl.ds(pl.multiple_of(q * quarter, quarter), quarter)
            total = dot_nn(hidden[0, at, :], matrix[0:hid2, cols])
            for s in range(1, ring):
                total = total + dot_nn(hidden[s, at, :], matrix[s * hid2 : (s + 1) * hid2, cols])
            if scaled:
                total = total * level_div[at, 0:1] * col_div[0:1, cols]
            total = total.astype(BF)
            head[h * half_head : (h + 1) * half_head, cols] = total[:half_head]
            order = (back_row & (turn_part == q)).astype(F32).astype(BF)
            rest_acc[...] += dot_nn(order, total[half_head:])
            return carry

        lax.fori_loop(0, 4, piece, 0)
        rest[h * half_head : (h + 1) * half_head, :] = rest_acc[...].astype(BF)

    def levels(h):
        def piece(i, carry):
            at = pl.ds(pl.multiple_of(h * half + i * strip, strip), strip)
            best = jnp.zeros((strip, hid2), F32)
            for s in range(ring):
                best = jnp.maximum(best, jnp.abs(hid_quant[s, at, :].astype(F32)))
            peak = jnp.max(best, axis=1, keepdims=True) + 1e-06
            mul = 7.0 / peak
            level_div[at, :] = jnp.broadcast_to(peak / 7.0, (strip, 128))
            for s in range(ring):
                hid_level[s, at, :] = soft_level(hid_quant[s, at, :].astype(F32) * mul).astype(BF)
            return carry

        lax.fori_loop(0, half // strip, piece, 0)

    use_float(x, 0, True)
    use_float(x, 1, True)
    for copy in peak_rows:
        copy.wait()
    best_row = row_peak[0]
    for s in range(1, ring):
        best_row = jnp.maximum(best_row, row_peak[s])
    for b in range(n_block):
        flat = jnp.broadcast_to(best_row[b : b + 1, :], (block, block))
        tall = jnp.sum(jnp.where(eye, flat, 0.0), axis=1, keepdims=True) + 1e-06
        row_mul[b * block : (b + 1) * block, :] = jnp.broadcast_to(7.0 / tall, (block, 128))
        row_div[b * block : (b + 1) * block, :] = jnp.broadcast_to(tall / 7.0, (block, 128))
    level_rows(x, 0, rows_q)
    use_quant(x, 0, True, rows_q)
    relay(3, rows, 0)
    launch(0, rows, 1, (1,))
    use_pair(0)
    use_across(0)
    activate(acc_float, hid_float, 0)
    launch(1, hid_float, 0, (0, 1))
    activate(acc_quant, hid_quant, 0)
    level_rows(x, 1, rows_q)
    use_quant(x, 1, True, rows_q)
    relay(1, hid_float, 0)
    launch(2, hid_quant, 0, (0, 1))
    relay(0, rows, 1)
    await_step(1, hid_float, 0, 1)
    await_step(1, hid_float, 0, 2)
    project(hid_float, down, outf_head, outf_rest, 0, False)
    send_back(1, 0, outf_head, outf_rest, backf_head, backf_rest)
    relay(2, hid_quant, 0)
    far_arrive()
    use_pair(1)
    await_step(2, hid_quant, 0, 1)
    await_step(2, hid_quant, 0, 2)
    use_across(1)
    activate(acc_float, hid_float, 1)
    launch(1, hid_float, 1, (0, 1))
    activate(acc_quant, hid_quant, 1)
    levels(0)
    relay(1, hid_float, 1)
    launch(2, hid_quant, 1, (0, 1))
    project(hid_level, down_q, outq_head, outq_rest, 0, True)
    send_back(2, 0, outq_head, outq_rest, backq_head, backq_rest)
    await_step(1, hid_float, 1, 1)
    await_step(1, hid_float, 1, 2)
    project(hid_float, down, outf_head, outf_rest, 1, False)
    send_back(1, 1, outf_head, outf_rest, backf_head, backf_rest)
    relay(2, hid_quant, 1)
    await_step(2, hid_quant, 1, 1)
    await_step(2, hid_quant, 1, 2)
    levels(1)
    project(hid_level, down_q, outq_head, outq_rest, 1, True)
    send_back(2, 1, outq_head, outq_rest, backq_head, backq_rest)
    sent_float = back(1, outf_head, outf_rest, backf_head, backf_rest)
    sent_quant = back(2, outq_head, outq_rest, backq_head, backq_rest)

    def combine(number, head, rest):
        mixed = dot_nn(mix_head[...], head[...])
        mixed = mixed[:toks] + mixed[toks:]
        quarter_of = (iota((2 * toks, n_head), 1) // REST) % 4
        for q in range(4):
            weights = jnp.where(quarter_of == q, mix_rest[...].astype(F32), 0.0).astype(BF)
            extra = dot_nn(weights, rest[...])
            cols = slice(q * quarter, (q + 1) * quarter)
            first = (q * quarter) // width
            inner = q * quarter - first * width
            part[number, first, :, inner : inner + quarter] = mixed[:, cols] + extra[:toks] + extra[toks:]
        copy = pltpu.make_async_remote_copy(
            src_ref=part.at[number, 1 - core],
            dst_ref=part_in.at[number],
            send_sem=ex_send.at[number],
            recv_sem=ex_recv.at[number],
            device_id=partner,
            device_id_type=MESH,
        )
        copy.start()
        return copy

    for copy in sent_float:
        copy.wait_recv()
    half_float = combine(0, backf_head, backf_rest)
    half_float.wait()
    both_ref[0] = part[0, core] + part_in[0]
    for copy in sent_quant:
        copy.wait_recv()
    half_quant = combine(1, backq_head, backq_rest)

    for copy in sent_float:
        copy.wait_send()
    for copy in sent_quant:
        copy.wait_send()

    @pl.when(odd)
    def _():
        for slot in range(ring - 1):
            far_copy(slot, far_head.at[slot, total, :], far_head.at[slot, total, :], 1).wait_send()
        far_copy(ring - 1, far_rest.at[total, :], far_rest.at[total, :], 1).wait_send()

    for number, ref in enumerate((rows, hid_float, hid_quant, rows)):
        drain(number, ref)
    half_quant.wait()
    both_ref[1] = part[1, core] + part_in[1]


def solution(mesh):
    groups = mesh.shape["dp"]
    ring = mesh.shape["expert"] // 2

    def on_device(tokens, expert_ids, route_weights, gate_weight, up_weight, down_weight):
        toks, width = tokens.shape
        wide = 2 * width
        quarter = wide // 4
        hid = gate_weight.shape[1]
        hid2 = 2 * hid
        count = groups * CAP
        half = count // 2
        n_head = groups * HEAD
        hidden_all = ring * hid2
        block = 128 if count % 128 == 0 else count
        vmem = pltpu.VMEM
        dma = pltpu.SemaphoreType.DMA
        here = pl.BlockSpec(memory_space=pltpu.VMEM)
        away = pl.BlockSpec(memory_space=pl.ANY)
        both = pl.pallas_call(
            functools.partial(layer_kernel, groups, ring),
            name="moe_layer",
            out_shape=jax.ShapeDtypeStruct((2, toks, width), F32),
            in_specs=[here, here, here, away, away, away],
            out_specs=here,
            scratch_shapes=[
                vmem((toks, wide), BF),
                vmem((n_head, wide), BF),
                vmem((n_head, quarter), BF),
                vmem((ring, count, wide), BF),
                vmem((n_head, quarter), BF),
                vmem((ring, 2 * hid2, wide), BF),
                vmem((ring, 2 * hid2, wide), BF),
                vmem((hidden_all, wide), BF),
                vmem((hidden_all, wide), BF),
                vmem((half, wide), BF),
                vmem((half, wide), BF),
                vmem((count, 2 * hid2), F32),
                vmem((count, 2 * hid2), F32),
                vmem((ring, count, hid2), BF),
                vmem((ring, count, hid2), BF),
                vmem((ring, count, hid2), BF),
                vmem((ring, 8, wide), F32),
                vmem((ring - 1, 8, wide), F32),
                vmem((ring, 8, wide), F32),
                vmem((ring, 8, wide), F32),
                vmem((ring, 8, block), F32),
                vmem((count, 128), F32),
                vmem((count, 128), F32),
                vmem((count, 128), F32),
                vmem((8, wide), F32),
                vmem((8, wide), F32),
                vmem((groups * (wide // 128), 128), F32),
                vmem((groups * (wide // 128), 128), F32),
                vmem((2 * toks, n_head), BF),
                vmem((2 * toks, n_head), BF),
                vmem((n_head, wide), BF),
                vmem((n_head, quarter), BF),
                vmem((n_head, wide), BF),
                vmem((n_head, quarter), BF),
                vmem((n_head // 2, quarter), F32),
                vmem((n_head, wide), BF),
                vmem((n_head, quarter), BF),
                vmem((n_head, wide), BF),
                vmem((n_head, quarter), BF),
                vmem((2, 2, toks, width), F32),
                vmem((2, toks, width), F32),
                vmem((ring - 1, toks, wide // 2), BF),
                vmem((ring - 1, n_head, wide // 2), BF),
                vmem((n_head, (ring - 1) * quarter // 2), BF),
                vmem((n_head // 2, (ring - 1) * quarter // 2), BF),
                dma((ring - 1,)),
                dma((ring - 1,)),
                dma((ring,)),
                dma((ring,)),
                dma((2 * ring + 1,)),
                dma((2 + 2 * ring,)),
                dma((2 + 2 * ring,)),
                dma((5, 2)),
                dma((5, 2)),
                dma((3, ring - 1)),
                dma((3, ring - 1)),
                dma((4, 2, 2, 3)),
                dma((4, 2, 2, 3)),
                dma((2,)),
                dma((2,)),
            ],
            compiler_params=pltpu.CompilerParams(
                collective_id=0, has_side_effects=True, vmem_limit_bytes=64 * 1024 * 1024 - 128 * 1024
            ),
        )(
            tokens,
            expert_ids.T,
            route_weights.T,
            gate_weight,
            up_weight,
            down_weight,
        )
        return both[1].astype(BF), both[0]

    in_specs = (
        P("dp", "expert"),
        P("dp", None),
        P("dp", None),
        P("dp", "expert", None),
        P("dp", "expert", None),
        P("dp", None, "expert"),
    )
    out_specs = (P("dp", "expert"), P("dp", "expert"))
    return jax.shard_map(
        on_device, mesh=mesh, in_specs=in_specs, out_specs=out_specs, check_vma=False
    )
```
